512 devices in a mesh: space: 16 (over y, x_hi, core), date: 32 (over x_lo, z).
Axes of the slice: x: 4 (x_hi: 2, x_lo: 2; x = x_hi * 2 + x_lo), y: 4, z: 16, core: 2. Of those that a mesh axis runs over, the one named last changes fastest.
Arguments:
- obs: bfloat16 [7, 768, 128, 512], P(None, 'date', 'space'), may hold values from -30 to 30
- valid: int32 [768, 128, 512], P('date', 'space'), may hold values from 0 to 1
- days: int32 [768], P('date'), may hold values from 0 to 3649, as said below
Outputs:
- coefficients: float32 [7, 8, 128, 512], P(None, None, 'space', 'date')
- noise_scale: float32 [128, 512], P('space', 'date')
The draws below stay inside these ranges and needn't reach their ends.
Inputs may be any that keep to these rules, and one draw needn't show every extreme that they name: `days`: day numbers of the acquisitions, in no particular order.
All inputs are finite; a program needn't handle non-finite values.
Results may differ from the reference program's by a relative error of at most 0.0003.
Values may be sent and summed in bfloat16 or wider, within the bound.
A program may use at most 128 MiB of HBM per device.

```python
import math
import jax
import jax.numpy as jnp
import numpy as np
from jax import lax

BANDS = 7
COLS = 512
ITERS = 2
DATES = 768
ROWS = 128


def shared_days(key):
    day_key = jax.random.fold_in(key, 11)
    drawn = jax.random.randint(day_key, (DATES,), 0, 3650, dtype=jnp.int32)
    return drawn.at[0].set(0).at[DATES - 1].set(3649)


def draw_days(key, part):
    return shared_days(key)


def draw_valid(key, part):
    days_now = shared_days(key)
    phase_shift = jax.random.randint(jax.random.fold_in(key, 81), (ROWS, COLS), 0, 365, dtype=jnp.int32)
    cloud_span = jax.random.randint(jax.random.fold_in(key, 91), (ROWS, COLS), 60, 181, dtype=jnp.int32)
    season_day = (days_now[:, None, None] + phase_shift[None]) % 365
    in_cloud = season_day < cloud_span[None]
    clear_odds = jnp.where(in_cloud, 25, 90)
    dice_roll = jax.random.randint(jax.random.fold_in(key, 101), (DATES, ROWS, COLS), 0, 100, dtype=jnp.int32)
    return jnp.where(dice_roll < clear_odds, 1, 0).astype(jnp.int32)


def draw_obs(key, part):
    day_float = shared_days(key).astype(jnp.float32)
    angle = day_float * (2.0 * math.pi / 365.25)
    basis = [jnp.ones_like(day_float), (day_float - 1825.0) / 1825.0]
    for harmonic in range(1, 4):
        basis.append(jnp.cos(harmonic * angle))
        basis.append(jnp.sin(harmonic * angle))
    coef_draw = jnp.clip(jax.random.normal(jax.random.fold_in(key, 21), (BANDS, 8, ROWS, COLS), jnp.float32), -4.0, 4.0) * 0.5
    signal = jnp.zeros((BANDS, DATES, ROWS, COLS), jnp.float32)
    for term in range(8):
        signal = signal + coef_draw[:, term][:, None] * basis[term][None, :, None, None]
    date_scale = jnp.exp(math.log(3.0) * jnp.arange(DATES, dtype=jnp.float32) / (DATES - 1))
    noise_key = jax.random.fold_in(key, 31)
    pixel_key = jax.random.fold_in(key, 41)
    noise = jnp.clip(jax.random.normal(noise_key, (BANDS, DATES, ROWS, COLS), jnp.float32), -6.0, 6.0)
    pixel_scale = jnp.exp(jax.random.uniform(pixel_key, (ROWS, COLS), jnp.float32, math.log(0.5), math.log(2.0)))
    hit_draw = jax.random.uniform(jax.random.fold_in(key, 51), (DATES, ROWS, COLS), jnp.float32)
    size_draw = jax.random.uniform(jax.random.fold_in(key, 61), (DATES, ROWS, COLS), jnp.float32, 8.0, 20.0)
    sign_draw = jax.random.uniform(jax.random.fold_in(key, 71), (DATES, ROWS, COLS), jnp.float32)
    hit_flag = jnp.where(hit_draw < 0.03, 1.0, 0.0)
    sign_flag = jnp.where(sign_draw < 0.7, 1.0, -1.0)
    offset = hit_flag * sign_flag * size_draw
    result = signal + 0.3 * noise * date_scale[None, :, None, None] * pixel_scale[None, None] + offset[None]
    return jnp.clip(result, -30.0, 30.0).astype(jnp.bfloat16)


def setup_inputs(seed: int = 0) -> dict:
    key_list = jax.random.split(jax.random.key(seed), 4)
    return {
        "obs": draw_obs(jax.random.fold_in(key_list[3], 71), 0),
        "valid": draw_valid(jax.random.fold_in(key_list[3], 71), 0),
        "days": draw_days(jax.random.fold_in(key_list[3], 71), 0),
    }


tukey_const = 4.685
ridge_value = 1.0
scale_eps = 1e-06
highest = lax.Precision.HIGHEST
pair_first = np.array([row_index for row_index in range(8) for col_index in range(row_index, 8)], dtype=np.int32)
pair_second = np.array([col_index for row_index in range(8) for col_index in range(row_index, 8)], dtype=np.int32)

def design(day_numbers):
    day_float = day_numbers.astype(jnp.float32)
    columns = [jnp.ones_like(day_float), (day_float - 1825.0) / 1825.0]
    angle = day_float * (2.0 * math.pi / 365.25)
    for harmonic in range(1, 4):
        columns.append(jnp.cos(harmonic * angle))
        columns.append(jnp.sin(harmonic * angle))
    return jnp.stack(columns, axis=1)

def box_sum(padded, row_count, col_count):
    across = padded[0:row_count]
    for offset in range(1, 5):
        across = across + padded[offset:offset + row_count]
    window_sum = across[:, 0:col_count]
    for offset in range(1, 5):
        window_sum = window_sum + across[:, offset:offset + col_count]
    return window_sum

def reference(obs, valid, days):
    design_rows = design(days)
    date_count = design_rows.shape[0]
    pixels = ROWS * COLS
    mask_float = valid.astype(jnp.float32).reshape(date_count, pixels)
    products = design_rows[:, pair_first] * design_rows[:, pair_second]
    counts = box_sum(jnp.pad(jnp.ones((ROWS, COLS), jnp.float32), 2), ROWS, COLS)
    weighted = mask_float
    for step in range(ITERS):
        gram_terms = jnp.dot(products.T.astype(jnp.float32), weighted.astype(jnp.float32), precision=highest, preferred_element_type=jnp.float32)
        crosses = []
        for band in range(BANDS):
            observed = obs[band].astype(jnp.float32).reshape(date_count, pixels)
            crosses.append(jnp.dot(design_rows.T.astype(jnp.float32), (weighted * observed).astype(jnp.float32), precision=highest, preferred_element_type=jnp.float32))
        full_gram = jnp.zeros((8, 8, pixels), jnp.float32)
        full_gram = full_gram.at[pair_first, pair_second].set(gram_terms)
        full_gram = full_gram.at[pair_second, pair_first].set(gram_terms)
        full_gram = full_gram + ridge_value * jnp.eye(8, dtype=jnp.float32)[:, :, None]
        right_sides = jnp.transpose(jnp.stack(crosses, axis=0), (2, 1, 0))
        solved = jnp.linalg.solve(jnp.transpose(full_gram, (2, 0, 1)), right_sides)
        coefficient = jnp.transpose(solved, (2, 1, 0))
        resid_power = jnp.zeros((date_count, pixels), jnp.float32)
        for band in range(BANDS):
            observed = obs[band].astype(jnp.float32).reshape(date_count, pixels)
            misfit = observed - jnp.dot(design_rows.astype(jnp.float32), coefficient[band].astype(jnp.float32), precision=highest, preferred_element_type=jnp.float32)
            resid_power = resid_power + misfit * misfit
        resid_power = resid_power / BANDS
        variance = lax.optimization_barrier(jnp.sum(weighted * resid_power, axis=0)) / (1.0 + gram_terms[0])
        smooth = (box_sum(jnp.pad(variance.reshape(ROWS, COLS), 2), ROWS, COLS) / counts).reshape(pixels)
        if step + 1 < ITERS:
            scaled = jnp.minimum(resid_power / (tukey_const * tukey_const * (smooth[None] + scale_eps)), 1.0)
            weighted = mask_float * (1.0 - scaled) * (1.0 - scaled)
    coefficients = coefficient.reshape(BANDS, 8, ROWS, COLS)
    noise_scale = jnp.sqrt(smooth + scale_eps).reshape(ROWS, COLS)
    return (coefficients, noise_scale)
```

```python
import functools
import math

import jax
import jax.numpy as jnp
from jax import lax
from jax.experimental import pallas as pl
from jax.experimental.pallas import tpu as pltpu
from jax.sharding import PartitionSpec as P

F32 = jnp.float32
MESH = pl.DeviceIdType.MESH
TUKEY = 4.685
EPS = 1e-06
BANDS = 7
TERMS = 8
ROWS = 8
COLS = 512
TILES = 4
SHARDS = 32
DEEP = 80
HALF = 40
BLOCK = 64
FIELDS = 24
ZS = 16

C0, S0, TC0, TS0, EXTRA_S = 2, 8, 14, 17, 21
NEIGHBOURS = [(a, b) for a in (-1, 0, 1) for b in (-1, 0, 1) if (a, b) != (0, 0)]


def extra_row(e):
    return 8 * e + 7 if e < 8 else 64 + e - 8


def gram_terms(i, j):
    if i > j:
        i, j = j, i
    if i == 0:
        if j < 2:
            return [(1.0, j)]
        n = j // 2
        return [(1.0, (C0 if j % 2 == 0 else S0) + n)]
    if i == 1:
        if j == 1:
            return [(1.0, 2)]
        n = j // 2
        return [(1.0, (TC0 if j % 2 == 0 else TS0) + n)]
    a, b = i // 2, j // 2

    def cosine(n):
        return 0 if n == 0 else C0 + n

    if i % 2 == 0 and j % 2 == 0:
        return [(0.5, cosine(abs(a - b))), (0.5, cosine(a + b))]
    if i % 2 == 1 and j % 2 == 1:
        return [(0.5, cosine(abs(a - b))), (-0.5, cosine(a + b))]
    s, c = (a, b) if i % 2 == 1 else (b, a)
    terms = [(0.5, S0 + s + c)]
    if s != c:
        terms.append((0.5 if s > c else -0.5, S0 + abs(s - c)))
    return terms


def design_table(days):
    day = days.astype(F32)
    angle = day * (2.0 * math.pi / 365.25)
    t = (day - 1825.0) / 1825.0
    c = [None] + [jnp.cos(h * angle) for h in range(1, 4)]
    s = [None] + [jnp.sin(h * angle) for h in range(1, 4)]
    c += [2 * c[2] * c[2] - 1, c[2] * c[3] - s[2] * s[3], 2 * c[3] * c[3] - 1]
    s += [2 * s[2] * c[2], s[2] * c[3] + c[2] * s[3], 2 * s[3] * c[3]]
    fields = [jnp.ones_like(t), t, t * t] + c[1:] + s[1:]
    fields += [t * c[h] for h in range(1, 4)] + [t * s[h] for h in range(1, 4)]
    fields += [jnp.zeros_like(t)] * (FIELDS - len(fields))
    table = jnp.stack(fields, axis=1)
    return jnp.broadcast_to(table.reshape(-1, 1), (table.size, 128))


COLUMN = [0, 1, C0 + 1, S0 + 1, C0 + 2, S0 + 2, C0 + 3, S0 + 3]


def flip_masks():
    sub = lax.broadcasted_iota(jnp.int32, (8, 128), 0)
    group = lax.broadcasted_iota(jnp.int32, (8, 128), 1) // 16
    masks = []
    for bit in (4, 2, 1):
        s, g = (sub & bit) != 0, (group & bit) != 0
        masks.append((jnp.logical_and(s, jnp.logical_not(g)), jnp.logical_and(jnp.logical_not(s), g)))
    return masks


def flip(v, masks):
    for bit, (low, high) in zip((4, 2, 1), masks):
        up = pltpu.roll(pltpu.roll(v, bit, 0), 128 - 16 * bit, 1)
        if bit == 4:
            v = jnp.where(jnp.logical_or(low, high), up, v)
        else:
            down = pltpu.roll(pltpu.roll(v, 8 - bit, 0), 16 * bit, 1)
            v = jnp.where(low, up, jnp.where(high, down, v))
    return v


def tile(q):
    return slice(128 * q, 128 * q + 128)


def splat(table_ref, d, field):
    return table_ref[pl.ds(d * FIELDS + field, 8, stride=0), :]


def form_moments(dates, load, w_ref, table_ref, s_ref, out_ref):
    masks = flip_masks()
    zero = jnp.zeros((8, 128), F32)

    def put(row, q, v):
        out_ref[pl.ds(q * 8 * DEEP + row, 8, stride=DEEP), :] = flip(v, masks)

    for b in range(BANDS):

        def body(d, carry):
            acc, square = list(carry[0]), list(carry[1])
            wy = []
            for q in range(TILES):
                y = load(b, d, q)
                v = w_ref[d, :, tile(q)] * y
                square[q] = square[q] + v * y
                wy.append(v)
            for k in range(TERMS):
                x = splat(table_ref, d, COLUMN[k])
                for q in range(TILES):
                    acc[k * TILES + q] = acc[k * TILES + q] + x * wy[q]
            return tuple(acc), tuple(square)

        acc, square = lax.fori_loop(
            0, dates, body, ((zero,) * (TERMS * TILES), (zero,) * TILES)
        )
        for k in range(TERMS):
            for q in range(TILES):
                put(8 * k + b, q, acc[k * TILES + q])
        for q in range(TILES):
            if b == 0:
                s_ref[:, tile(q)] = square[q]
            else:
                s_ref[:, tile(q)] = s_ref[:, tile(q)] + square[q]
    for first in range(0, EXTRA_S, 7):
        fields = list(range(first, min(first + 7, EXTRA_S)))

        def body(d, acc):
            acc = list(acc)
            w = [w_ref[d, :, tile(q)] for q in range(TILES)]
            for n, e in enumerate(fields):
                if e == 0:
                    for q in range(TILES):
                        acc[q] = acc[q] + w[q]
                    continue
                x = splat(table_ref, d, e)
                for q in range(TILES):
                    acc[n * TILES + q] = acc[n * TILES + q] + x * w[q]
            return tuple(acc)

        acc = lax.fori_loop(0, dates, body, (zero,) * (len(fields) * TILES))
        for n, e in enumerate(fields):
            for q in range(TILES):
                put(extra_row(e), q, acc[n * TILES + q])
    for q in range(TILES):
        put(extra_row(EXTRA_S), q, s_ref[:, tile(q)])
        for row in range(extra_row(EXTRA_S) + 1, DEEP):
            out_ref[pl.ds(q * 8 * DEEP + row, 8, stride=DEEP), :] = zero


def first_kernel(dates, obs_ref, valid_ref, table_ref, out_ref, w_ref, s_ref):
    @pl.loop(0, dates)
    def _(d):
        w_ref[d] = valid_ref[d].astype(F32)

    form_moments(
        dates, lambda b, d, q: obs_ref[b, d, :, tile(q)].astype(F32), w_ref, table_ref, s_ref, out_ref
    )


def second_kernel(
    dates, obs_ref, valid_ref, table_ref, block_ref, out_ref, beta_ref, r_ref, w_ref, s_ref
):
    masks = flip_masks()

    def get(row, q):
        return flip(block_ref[pl.ds(q * 8 * BLOCK + row, 8, stride=BLOCK), :], masks)

    for b in range(BANDS):
        beta = [[get(8 * k + b, q) for q in range(TILES)] for k in range(TERMS)]

        def body(d, carry):
            x = [splat(table_ref, d, COLUMN[k]) for k in range(TERMS)]
            for q in range(TILES):
                fit = beta[0][q]
                for k in range(1, TERMS):
                    fit = fit + x[k] * beta[k][q]
                r = obs_ref[b, d, :, tile(q)].astype(F32) - fit
                r_ref[b, d, :, tile(q)] = r
                if b == 0:
                    w_ref[d, :, tile(q)] = r * r
                else:
                    w_ref[d, :, tile(q)] = w_ref[d, :, tile(q)] + r * r
            return carry

        lax.fori_loop(0, dates, body, 0)
    scale = [1.0 / (float(BANDS) * (TUKEY * TUKEY) * (get(7, q) + EPS)) for q in range(TILES)]

    @pl.loop(0, dates)
    def _(d):
        for q in range(TILES):
            left = 1.0 - jnp.minimum(w_ref[d, :, tile(q)] * scale[q], 1.0)
            w_ref[d, :, tile(q)] = valid_ref[d, :, tile(q)].astype(F32) * left * left

    form_moments(
        dates, lambda b, d, q: r_ref[b, d, :, tile(q)], w_ref, table_ref, s_ref, out_ref
    )


def copy_to(src, dst, send, recv, space, date):
    return pltpu.make_async_remote_copy(
        src_ref=src, dst_ref=dst, send_sem=send, recv_sem=recv, device_id=(space, date), device_id_type=MESH
    )


def place():
    s, j = lax.axis_index("space"), lax.axis_index("date")
    return s, j, j // ZS, lax.rem(j, ZS)


def wrap(value, count):
    return lax.rem(value + count, count)


def barrier():
    s, j, x, z = place()
    sem = pltpu.get_barrier_semaphore()
    targets = [(s, x * ZS + wrap(z + 1, ZS)), (s, x * ZS + wrap(z - 1, ZS)), (s, (1 - x) * ZS + z)]
    targets += [(wrap(s + a, 16), wrap(j + b, SHARDS)) for a, b in NEIGHBOURS]
    for target in targets:
        pl.semaphore_signal(sem, inc=1, device_id=target, device_id_type=MESH)
    pl.semaphore_wait(sem, len(targets))


def reduce_scatter(mom_ref, slot_ref, mine_ref, other_ref, landed_ref, sems):
    ring_send, ring_recv, x_send, x_recv = sems
    s, j, x, z = place()
    to = [(s, x * ZS + wrap(z + 1, ZS)), (s, x * ZS + wrap(z - 1, ZS))]
    side = [1 - x, 1 - x, x, x]

    def rows(shard_z, ch):
        start = (side[ch] * ZS + shard_z) * DEEP + HALF * (ch % 2)
        return pl.ds(pl.multiple_of(start, 8), HALF)

    def target(way, step):
        return wrap(z + 8 - step, ZS) if way == 0 else wrap(z - 7 + step, ZS)

    def hop(way, step, ch, src):
        return copy_to(
            src, slot_ref.at[way, step, ch], ring_send.at[way, step, ch], ring_recv.at[way, step, ch], *to[way]
        )

    for ch in range(4):
        for way in range(2):
            hop(way, 0, ch, mom_ref.at[rows(target(way, 0), ch)]).start()

    def add(way, step, ch):
        hop(way, step - 1, ch, slot_ref.at[way, step - 1, ch]).wait_recv()
        slot_ref[way, step - 1, ch] = slot_ref[way, step - 1, ch] + mom_ref[rows(target(way, step), ch), :]
        hop(way, step, ch, slot_ref.at[way, step - 1, ch]).start()

    def body(step, carry):
        for ch in range(4):
            add(0, step, ch)
            add(1, step, ch)
        return carry

    lax.fori_loop(1, 7, body, 0)
    for ch in range(4):
        add(0, 7, ch)
    swaps = []
    for ch in range(4):
        hop(0, 7, ch, slot_ref.at[0, 7, ch]).wait_recv()
        hop(1, 6, ch, slot_ref.at[1, 6, ch]).wait_recv()
        total = mom_ref[rows(z, ch), :] + slot_ref[0, 7, ch] + slot_ref[1, 6, ch]
        if ch < 2:
            other_ref[ch] = total
            swap = copy_to(
                other_ref.at[ch], landed_ref.at[ch], x_send.at[ch], x_recv.at[ch], s, (1 - x) * ZS + z
            )
            swap.start()
            swaps.append(swap)
        else:
            h = ch - 2
            swaps[h].wait_recv()
            mine_ref[HALF * h : HALF * h + HALF, :] = total + landed_ref[h]
    for swap in swaps:
        swap.wait_send()

    def drain(step, carry):
        for ch in range(4):
            hop(0, step, ch, slot_ref.at[0, step, ch]).wait_send()
            hop(1, step, ch, slot_ref.at[1, step, ch]).wait_send()
        return carry

    lax.fori_loop(0, 7, drain, 0)
    for ch in range(4):
        hop(0, 7, ch, slot_ref.at[0, 7, ch]).wait_send()


def solve(mine_ref, base):
    moment = {}

    def mom(e):
        if e not in moment:
            moment[e] = jnp.broadcast_to(mine_ref[extra_row(e) : extra_row(e) + 1, :], (8, 128))
        return moment[e]

    gram = {}
    for i in range(TERMS):
        for j in range(i, TERMS):
            value = None
            for factor, e in gram_terms(i, j):
                part = mom(e) if factor == 1.0 else factor * mom(e)
                value = part if value is None else value + part
            gram[i, j] = value
    cross = [mine_ref[8 * k : 8 * k + 8, :] for k in range(TERMS)]
    work = dict(gram)
    for i in range(TERMS):
        work[i, i] = work[i, i] + 1.0
    right = [cross[k] if base is None else cross[k] - base[k] for k in range(TERMS)]
    inverse, factor = [], {}
    for i in range(TERMS):
        inv = 1.0 / work[i, i]
        inverse.append(inv)
        for r in range(i + 1, TERMS):
            factor[r, i] = work[i, r] * inv
        for r in range(i + 1, TERMS):
            for c in range(r, TERMS):
                work[r, c] = work[r, c] - factor[r, i] * work[i, c]
            right[r] = right[r] - factor[r, i] * right[i]
    answer = [None] * TERMS
    for i in reversed(range(TERMS)):
        value = right[i] * inverse[i]
        for c in range(i + 1, TERMS):
            value = value - factor[c, i] * answer[c]
        answer[i] = value
    lost = None
    for i in range(TERMS):
        image = None
        for c in range(TERMS):
            part = gram[min(i, c), max(i, c)] * answer[c]
            image = part if image is None else image + part
        part = answer[i] * (2.0 * cross[i] - image)
        lost = part if lost is None else lost + part
    sub = lax.broadcasted_iota(jnp.int32, (8, 128), 0)
    lost = jnp.sum(jnp.where(sub < BANDS, lost, 0.0), axis=0, keepdims=True)
    spread = jnp.maximum(mom(EXTRA_S) - jnp.broadcast_to(lost, (8, 128)), 0.0) * (1.0 / BANDS)
    return answer, spread / (1.0 + mom(0))


def swap_halo(variance, own_ref, near_ref, sems):
    send, recv = sems
    s, j, x, z = place()
    own_ref[...] = variance
    copies = []
    for n, (a, b) in enumerate(NEIGHBOURS):
        back = NEIGHBOURS.index((-a, -b))
        copy = copy_to(
            own_ref, near_ref.at[back], send.at[n], recv.at[back], wrap(s + a, 16), wrap(j + b, SHARDS)
        )
        copy.start()
        copies.append(copy)
    return copies


def box_mean(variance, near_ref, copies):
    s, j, x, z = place()
    for copy in copies:
        copy.wait()
    lane = lax.broadcasted_iota(jnp.int32, (8, 128), 1)
    col, row = lane % 16, lane // 16

    def field(a, b):
        if (a, b) == (0, 0):
            return variance
        value = near_ref[NEIGHBOURS.index((a, b))]
        inside = jnp.int32(1)
        if a:
            inside = inside * ((s + a >= 0) & (s + a < 16)).astype(jnp.int32)
        if b:
            inside = inside * ((j + b >= 0) & (j + b < SHARDS)).astype(jnp.int32)
        return jnp.where(jnp.full((8, 128), inside) > 0, value, 0.0)

    across = []
    for a in (-1, 0, 1):
        middle = field(a, 0)
        left = pltpu.roll(field(a, -1), 128 - 16, 1)
        right = pltpu.roll(field(a, 1), 16, 1)
        total = middle
        for step in (1, 2):
            total = total + pltpu.roll(jnp.where(col < step, right, middle), 128 - step, 1)
            total = total + pltpu.roll(jnp.where(col >= 16 - step, left, middle), step, 1)
        across.append(total)
    up, middle, down = across
    total = middle
    for step in (1, 2):
        total = total + pltpu.roll(jnp.where(row < step, down, middle), 128 - 16 * step, 1)
        total = total + pltpu.roll(jnp.where(row >= 8 - step, up, middle), 16 * step, 1)

    def count(index, whole):
        return (jnp.minimum(index + 2, whole - 1) - jnp.maximum(index - 2, 0) + 1).astype(F32)

    return total / (count(s * 8 + row, 128) * count(j * 16 + col, COLS))


def first_exchange(
    mom_ref, out_ref, slot_ref, mine_ref, other_ref, landed_ref, own_ref, near_ref,
    ring_send, ring_recv, x_send, x_recv, h_send, h_recv, g_send, g_recv, gx_send, gx_recv,
):
    s, j, x, z = place()
    barrier()
    reduce_scatter(mom_ref, slot_ref, mine_ref, other_ref, landed_ref, (ring_send, ring_recv, x_send, x_recv))
    answer, variance = solve(mine_ref, None)
    copies = swap_halo(variance, own_ref, near_ref, (h_send, h_recv))
    to = [(s, x * ZS + wrap(z + 1, ZS)), (s, x * ZS + wrap(z - 1, ZS))]
    side = [x, x, 1 - x, 1 - x]
    size = BLOCK // 2

    def part(owner_z, ch):
        start = (side[ch] * ZS + owner_z) * BLOCK + size * (1 - ch % 2)
        return out_ref.at[pl.ds(pl.multiple_of(start, 8), size)]

    def owner(way, step):
        return wrap(z - step, ZS) if way == 0 else wrap(z + step, ZS)

    def hop(way, step, ch):
        piece = part(owner(way, step), ch)
        return copy_to(piece, piece, g_send.at[way, step, ch], g_recv.at[way, step, ch], *to[way])

    def arrived(way, step, ch):
        piece = part(owner(way, step + 1), ch)
        copy_to(piece, piece, g_send.at[way, step, ch], g_recv.at[way, step, ch], *to[way]).wait_recv()

    def cross(ch, source):
        start = (source * ZS + z) * BLOCK + size * (1 - ch % 2)
        piece = out_ref.at[pl.ds(pl.multiple_of(start, 8), size)]
        return copy_to(piece, piece, gx_send.at[ch], gx_recv.at[ch], s, (1 - x) * ZS + z)

    sub = lax.broadcasted_iota(jnp.int32, (8, 128), 0)
    base = j * BLOCK
    for k in range(4, TERMS):
        out_ref[pl.ds(pl.multiple_of(base + 8 * k, 8), 8), :] = jnp.where(sub < BANDS, answer[k], 0.0)
    cross(0, x).start()
    for way in range(2):
        hop(way, 0, 0).start()
    smooth = box_mean(variance, near_ref, copies)
    for k in range(4):
        out_ref[pl.ds(pl.multiple_of(base + 8 * k, 8), 8), :] = jnp.where(sub < BANDS, answer[k], smooth)
    cross(1, x).start()
    for way in range(2):
        hop(way, 0, 1).start()
    for ch in range(2):
        cross(ch, 1 - x).wait_recv()
        for way in range(2):
            hop(way, 0, 2 + ch).start()

    def body(step, carry):
        for ch in range(4):
            for way in range(2):
                arrived(way, step - 1, ch)
                hop(way, step, ch).start()
        return carry

    lax.fori_loop(1, 7, body, 0)
    for ch in range(4):
        arrived(0, 6, ch)
        hop(0, 7, ch).start()
    for ch in range(4):
        arrived(1, 6, ch)
    for ch in range(4):
        arrived(0, 7, ch)
    for ch in range(2):
        cross(ch, x).wait_send()

    def drain(step, carry):
        for ch in range(4):
            for way in range(2):
                hop(way, step, ch).wait_send()
        return carry

    lax.fori_loop(0, 7, drain, 0)
    for ch in range(4):
        hop(0, 7, ch).wait_send()


def second_exchange(
    mom_ref, block_ref, coef_ref, noise_ref, slot_ref, mine_ref, other_ref, landed_ref, own_ref, near_ref,
    ring_send, ring_recv, x_send, x_recv, h_send, h_recv,
):
    s, j, x, z = place()
    barrier()
    reduce_scatter(mom_ref, slot_ref, mine_ref, other_ref, landed_ref, (ring_send, ring_recv, x_send, x_recv))
    base = [block_ref[pl.ds(pl.multiple_of(j * BLOCK + 8 * k, 8), 8), :] for k in range(TERMS)]
    answer, variance = solve(mine_ref, base)
    copies = swap_halo(variance, own_ref, near_ref, (h_send, h_recv))
    masks = flip_masks()
    for k in range(TERMS):
        spread = flip(base[k] + answer[k], masks)
        for b in range(BANDS):
            turned = spread if b == 0 else pltpu.roll(spread, 128 - 16 * b, 1)
            coef_ref[b, k] = turned[:, :16]
    smooth = box_mean(variance, near_ref, copies)
    noise_ref[...] = flip(jnp.sqrt(smooth + EPS), masks)[:, :16]


def exchange_scratch():
    ring = pltpu.SemaphoreType.DMA((2, 8, 4))
    two, eight = pltpu.SemaphoreType.DMA((2,)), pltpu.SemaphoreType.DMA((8,))
    return [
        pltpu.VMEM((2, 8, 4, HALF, 128), F32),
        pltpu.VMEM((DEEP, 128), F32),
        pltpu.VMEM((2, HALF, 128), F32),
        pltpu.VMEM((2, HALF, 128), F32),
        pltpu.VMEM((8, 128), F32),
        pltpu.VMEM((8, 8, 128), F32),
        ring, ring, two, two, eight, eight,
    ]


def vmem(count):
    return [pl.BlockSpec(memory_space=pltpu.VMEM)] * count


def on_device(obs, valid, days):
    dates = obs.shape[1]
    table = design_table(days)
    moments = jax.ShapeDtypeStruct((SHARDS * DEEP, 128), F32)
    weights = pltpu.VMEM((dates, ROWS, COLS), F32)
    squares = pltpu.VMEM((ROWS, COLS), F32)
    params = pltpu.CompilerParams(vmem_limit_bytes=48 << 20)
    first = pl.pallas_call(
        functools.partial(first_kernel, dates),
        out_shape=moments,
        in_specs=vmem(3),
        out_specs=vmem(1)[0],
        scratch_shapes=[weights, squares],
        compiler_params=params,
    )(obs, valid, table)
    ring = pltpu.SemaphoreType.DMA((2, 8, 4))
    two = pltpu.SemaphoreType.DMA((2,))
    block = pl.pallas_call(
        first_exchange,
        out_shape=jax.ShapeDtypeStruct((SHARDS * BLOCK, 128), F32),
        in_specs=vmem(1),
        out_specs=vmem(1)[0],
        scratch_shapes=exchange_scratch() + [ring, ring, two, two],
        compiler_params=pltpu.CompilerParams(collective_id=0, has_side_effects=True, vmem_limit_bytes=48 << 20),
    )(first)
    second = pl.pallas_call(
        functools.partial(second_kernel, dates),
        out_shape=moments,
        in_specs=vmem(4),
        out_specs=vmem(1)[0],
        scratch_shapes=[
            pltpu.VMEM((BANDS * TERMS, ROWS, 128), F32),
            pltpu.VMEM((BANDS, dates, ROWS, COLS), F32),
            weights,
            squares,
        ],
        compiler_params=params,
    )(obs, valid, table, block)
    return pl.pallas_call(
        second_exchange,
        out_shape=(
            jax.ShapeDtypeStruct((BANDS, TERMS, ROWS, 16), F32),
            jax.ShapeDtypeStruct((ROWS, 16), F32),
        ),
        in_specs=vmem(2),
        out_specs=tuple(vmem(2)),
        scratch_shapes=exchange_scratch(),
        compiler_params=pltpu.CompilerParams(collective_id=1, has_side_effects=True, vmem_limit_bytes=48 << 20),
    )(second, block)


def solution(mesh):
    in_specs = (P(None, "date", "space", None), P("date", "space", None), P("date"))
    out_specs = (P(None, None, "space", "date"), P("space", "date"))
    return jax.shard_map(on_device, mesh=mesh, in_specs=in_specs, out_specs=out_specs, check_vma=False)
```

```python
import functools
import math

import jax
import jax.numpy as jnp
from jax import lax
from jax.experimental import pallas as pl
from jax.experimental.pallas import tpu as pltpu
from jax.sharding import PartitionSpec as P

F32 = jnp.float32
MESH = pl.DeviceIdType.MESH
TUKEY = 4.685
EPS = 1e-06
BANDS = 7
TERMS = 8
ROWS = 8
COLS = 512
TILES = 4
SHARDS = 32
DEEP = 80
BLOCK = 64
FIELDS = 24
ZS = 16

C0, S0, TC0, TS0, EXTRA_S = 2, 8, 14, 17, 21
NEIGHBOURS = [(a, b) for a in (-1, 0, 1) for b in (-1, 0, 1) if (a, b) != (0, 0)]


PIECES = ((0, 16), (16, 24), (40, 16), (56, 24))
CHAINS = ((1, 8), (1, 7), (-1, 7), (-1, 6))
SPREADS = ((1, 2, 4), (1, 1, 4), (-1, 1, 4), (-1, 2, 3))
PARTS = ((0, 32), (32, 24), (56, 8))


def extra_row(e):
    return 8 * BANDS + e


def gram_terms(i, j):
    if i > j:
        i, j = j, i
    if i == 0:
        if j < 2:
            return [(1.0, j)]
        n = j // 2
        return [(1.0, (C0 if j % 2 == 0 else S0) + n)]
    if i == 1:
        if j == 1:
            return [(1.0, 2)]
        n = j // 2
        return [(1.0, (TC0 if j % 2 == 0 else TS0) + n)]
    a, b = i // 2, j // 2

    def cosine(n):
        return 0 if n == 0 else C0 + n

    if i % 2 == 0 and j % 2 == 0:
        return [(0.5, cosine(abs(a - b))), (0.5, cosine(a + b))]
    if i % 2 == 1 and j % 2 == 1:
        return [(0.5, cosine(abs(a - b))), (-0.5, cosine(a + b))]
    s, c = (a, b) if i % 2 == 1 else (b, a)
    terms = [(0.5, S0 + s + c)]
    if s != c:
        terms.append((0.5 if s > c else -0.5, S0 + abs(s - c)))
    return terms


def design_table(dates, days_ref, table_ref):
    rows = lax.broadcasted_iota(jnp.int32, (dates, 128), 0)
    day = jnp.zeros((dates, 128), F32)
    for d in range(dates):
        day = jnp.where(rows == d, days_ref[d].astype(F32), day)
    angle = day * (2.0 * math.pi / 365.25)
    t = (day - 1825.0) / 1825.0
    c = [None] + [jnp.cos(h * angle) for h in range(1, 4)]
    s = [None] + [jnp.sin(h * angle) for h in range(1, 4)]
    c += [2 * c[2] * c[2] - 1, c[2] * c[3] - s[2] * s[3], 2 * c[3] * c[3] - 1]
    s += [2 * s[2] * c[2], s[2] * c[3] + c[2] * s[3], 2 * s[3] * c[3]]
    fields = [jnp.ones_like(t), t, t * t] + c[1:] + s[1:]
    fields += [t * c[h] for h in range(1, 4)] + [t * s[h] for h in range(1, 4)]
    for f, value in enumerate(fields):
        for first in range(0, dates, 8):
            table_ref[pl.ds(first * FIELDS + f, 8, stride=FIELDS), :] = value[first : first + 8]


COLUMN = [0, 1, C0 + 1, S0 + 1, C0 + 2, S0 + 2, C0 + 3, S0 + 3]


def flip_masks():
    sub = lax.broadcasted_iota(jnp.int32, (8, 128), 0)
    group = lax.broadcasted_iota(jnp.int32, (8, 128), 1) // 16
    masks = []
    for bit in (4, 2, 1):
        s, g = (sub & bit) != 0, (group & bit) != 0
        masks.append((jnp.logical_and(s, jnp.logical_not(g)), jnp.logical_and(jnp.logical_not(s), g)))
    return masks


def flip(v, masks):
    for bit, (low, high) in zip((4, 2, 1), masks):
        up = pltpu.roll(pltpu.roll(v, bit, 0), 128 - 16 * bit, 1)
        if bit == 4:
            v = jnp.where(jnp.logical_or(low, high), up, v)
        else:
            down = pltpu.roll(pltpu.roll(v, 8 - bit, 0), 16 * bit, 1)
            v = jnp.where(low, up, jnp.where(high, down, v))
    return v


def tile(q):
    return slice(128 * q, 128 * q + 128)


def splat(table_ref, d, field):
    return table_ref[pl.ds(d * FIELDS + field, 8, stride=0), :]


def form_moments(dates, load, w_ref, table_ref, s_ref, out_refs, ready, done):
    masks = flip_masks()
    zero = jnp.zeros((8, 128), F32)

    def put(row, q, v):
        for (first, count), out_ref in zip(PIECES, out_refs):
            if first <= row < first + count:
                out_ref[pl.ds(q * 8 * count + row - first, 8, stride=count), :] = v

    def finish(row):
        for n, (first, count) in enumerate(PIECES):
            if row == first + count:
                done(n)

    for b in range(BANDS):
        ready(b)

        def body(d, carry):
            acc, square = list(carry[0]), list(carry[1])
            wy = []
            for q in range(TILES):
                y = load(b, d, q)
                v = w_ref[d, :, tile(q)] * y
                square[q] = square[q] + v * y
                wy.append(v)
            for k in range(TERMS):
                x = splat(table_ref, d, COLUMN[k]) if k else None
                for q in range(TILES):
                    acc[k * TILES + q] = acc[k * TILES + q] + (x * wy[q] if k else wy[q])
            return tuple(acc), tuple(square)

        acc, square = lax.fori_loop(
            0, dates, body, ((zero,) * (TERMS * TILES), (zero,) * TILES)
        )
        for k in range(TERMS):
            for q in range(TILES):
                put(8 * b + k, q, flip(acc[k * TILES + q], masks))
        for q in range(TILES):
            if b == 0:
                s_ref[:, tile(q)] = square[q]
            else:
                s_ref[:, tile(q)] = s_ref[:, tile(q)] + square[q]
        finish(8 * b + 8)
    for first in range(0, EXTRA_S, 7):
        fields = list(range(first, min(first + 7, EXTRA_S)))

        def body(d, acc):
            acc = list(acc)
            w = [w_ref[d, :, tile(q)] for q in range(TILES)]
            for n, e in enumerate(fields):
                x = splat(table_ref, d, e) if e else None
                for q in range(TILES):
                    acc[n * TILES + q] = acc[n * TILES + q] + (x * w[q] if e else w[q])
            return tuple(acc)

        acc = lax.fori_loop(0, dates, body, (zero,) * (len(fields) * TILES))
        for n, e in enumerate(fields):
            for q in range(TILES):
                put(extra_row(e), q, flip(acc[n * TILES + q], masks))
    for q in range(TILES):
        put(extra_row(EXTRA_S), q, flip(s_ref[:, tile(q)], masks))
        for row in range(extra_row(EXTRA_S) + 1, DEEP):
            put(row, q, zero)
    finish(DEEP)


def form_residuals(dates, obs_ref, valid_ref, table_ref, block_ref, r_ref, w_ref):
    masks = flip_masks()

    def get(row, q):
        return flip(block_ref[pl.ds(q * 8 * BLOCK + row, 8, stride=BLOCK), :], masks)

    for b in range(BANDS):
        beta = [[get(8 * b + k, q) for q in range(TILES)] for k in range(TERMS)]

        def body(d, carry):
            x = [splat(table_ref, d, COLUMN[k]) if k else None for k in range(TERMS)]
            for q in range(TILES):
                fit = beta[0][q]
                for k in range(1, TERMS):
                    fit = fit + x[k] * beta[k][q]
                r = obs_ref[b, d, :, tile(q)].astype(F32) - fit
                r_ref[b, d, :, tile(q)] = r
                if b == 0:
                    w_ref[d, :, tile(q)] = r * r
                else:
                    w_ref[d, :, tile(q)] = w_ref[d, :, tile(q)] + r * r
            return carry

        lax.fori_loop(0, dates, body, 0)
    scale = [1.0 / (float(BANDS) * (TUKEY * TUKEY) * (get(8 * BANDS, q) + EPS)) for q in range(TILES)]

    @pl.loop(0, dates)
    def _(d):
        for q in range(TILES):
            left = 1.0 - jnp.minimum(w_ref[d, :, tile(q)] * scale[q], 1.0)
            w_ref[d, :, tile(q)] = valid_ref[d, :, tile(q)].astype(F32) * left * left


def copy_to(src, dst, send, recv, space, date):
    return pltpu.make_async_remote_copy(
        src_ref=src, dst_ref=dst, send_sem=send, recv_sem=recv, device_id=(space, date), device_id_type=MESH
    )


def place():
    s, j = lax.axis_index("space"), lax.axis_index("date")
    return s, j, j // ZS, lax.rem(j, ZS)


def wrap(value, count):
    return lax.rem(value + count, count)


def greet():
    s, j, x, z = place()
    sem = pltpu.get_barrier_semaphore()
    targets = [(s, x * ZS + wrap(z + h, ZS)) for h in (1, -1, 2, -2)] + [(s, (1 - x) * ZS + z)]
    targets += [(wrap(s + a, 16), wrap(j + b, SHARDS)) for a, b in NEIGHBOURS]
    for target in targets:
        pl.semaphore_signal(sem, inc=1, device_id=target, device_id_type=MESH)
    return sem, len(targets)


class Reduction:
    def __init__(self, mom_refs, land_refs, slot_ref, mine_ref, sems):
        self.mom, self.land, self.slot, self.mine = mom_refs, land_refs, slot_ref, mine_ref
        self.x_send, self.x_recv, self.send, self.recv = sems
        self.s, self.j, self.x, self.z = place()

    def swap(self, n):
        size = ZS * PIECES[n][1]
        other = pl.multiple_of((1 - self.x) * size, 8)
        return copy_to(
            self.mom[n].at[pl.ds(other, size)], self.land[n], self.x_send.at[n], self.x_recv.at[n],
            self.s, (1 - self.x) * ZS + self.z,
        )

    def landed(self, n):
        self.swap(n).wait_recv()
        size = ZS * PIECES[n][1]
        own = pl.multiple_of(self.x * size, 8)
        self.land[n][...] = self.land[n][...] + self.mom[n][pl.ds(own, size), :]

    def length(self, chain):
        return (CHAINS[chain][1] + 1) // 2

    def rows(self, n, chain, step):
        way, first = CHAINS[chain]
        count = PIECES[n][1]
        return pl.ds(pl.multiple_of(wrap(self.z + way * (first - 2 * step), ZS) * count, 8), count)

    def place_of(self, n, chain, step):
        return self.slot.at[chain, step, pl.ds(*PIECES[n])]

    def hop(self, n, chain, step):
        way, first = CHAINS[chain]
        reach = min(2, first - 2 * step)
        source = self.land[n].at[self.rows(n, chain, 0)] if step == 0 else self.place_of(n, chain, step - 1)
        return copy_to(
            source, self.place_of(n, chain, step), self.send.at[chain, step, n], self.recv.at[chain, step, n],
            self.s, self.x * ZS + wrap(self.z + way * reach, ZS),
        )

    def step(self, n, step):
        for chain in range(4):
            if step >= self.length(chain):
                continue
            if step:
                self.hop(n, chain, step - 1).wait_recv()
                here = self.place_of(n, chain, step - 1)
                here[...] = here[...] + self.land[n][self.rows(n, chain, step), :]
            self.hop(n, chain, step).start()

    def finish(self, n):
        first, count = PIECES[n]
        total = self.land[n][pl.ds(pl.multiple_of(self.z * count, 8), count), :]
        for chain in range(4):
            last = self.length(chain) - 1
            self.hop(n, chain, last).wait_recv()
            total = total + self.slot[chain, last, pl.ds(first, count), :]
        self.mine[pl.ds(first, count), :] = total

    def run(self):
        count = len(PIECES)
        for wave in range(count + 4):
            for n in range(count):
                step = wave - n
                if step == 0:
                    self.landed(n)
                if 0 <= step < 4:
                    self.step(n, step)
                if step == 4:
                    self.finish(n)

    def drain(self):
        for n in range(len(PIECES)):
            self.swap(n).wait_send()
            for chain in range(4):
                for step in range(self.length(chain)):
                    self.hop(n, chain, step).wait_send()


class Spread:
    def __init__(self, block_ref, sems):
        self.block = block_ref
        self.send, self.recv, self.x_send, self.x_recv, self.own_send, self.own_recv = sems
        self.s, self.j, self.x, self.z = place()

    def piece(self, side, owner, n):
        first, count = PARTS[n]
        start = (side * ZS + wrap(owner + ZS, ZS)) * BLOCK + first
        return self.block.at[pl.ds(pl.multiple_of(start, 8), count)]

    def offset(self, chain, step):
        way, first, _ = SPREADS[chain]
        return 0 if step == 0 else way * (first + 2 * (step - 1))

    def hop(self, n, chain, step):
        way, first, _ = SPREADS[chain]
        reach = first if step == 0 else 2
        piece = self.piece(self.x, self.z - self.offset(chain, step), n)
        return copy_to(
            piece, piece, self.send.at[chain, step, n], self.recv.at[chain, step, n],
            self.s, self.x * ZS + wrap(self.z + way * reach, ZS),
        )

    def arrival(self, n, chain, step):
        piece = self.piece(self.x, self.z - self.offset(chain, step + 1), n)
        return copy_to(
            piece, piece, self.send.at[chain, step, n], self.recv.at[chain, step, n], self.s, self.j
        )

    def across(self, n, chain, step, side):
        piece = self.piece(side, self.z - self.offset(chain, step + 1), n)
        return copy_to(
            piece, piece, self.x_send.at[chain, step, n], self.x_recv.at[chain, step, n],
            self.s, (1 - self.x) * ZS + self.z,
        )

    def own_across(self, n, side):
        piece = self.piece(side, self.z, n)
        return copy_to(
            piece, piece, self.own_send.at[n], self.own_recv.at[n], self.s, (1 - self.x) * ZS + self.z
        )

    def begin(self, n):
        for chain in range(4):
            self.hop(n, chain, 0).start()
        self.own_across(n, self.x).start()

    def relay(self, step):
        for n in range(len(PARTS)):
            for chain in range(4):
                if step <= SPREADS[chain][2]:
                    self.arrival(n, chain, step - 1).wait_recv()
                    if step < SPREADS[chain][2]:
                        self.hop(n, chain, step).start()
                    self.across(n, chain, step - 1, self.x).start()

    def receive(self):
        for n in range(len(PARTS)):
            self.own_across(n, 1 - self.x).wait_recv()
            for chain in range(4):
                for step in range(SPREADS[chain][2]):
                    self.across(n, chain, step, 1 - self.x).wait_recv()

    def drain(self):
        for n in range(len(PARTS)):
            self.own_across(n, self.x).wait_send()
            for chain in range(4):
                for step in range(SPREADS[chain][2]):
                    self.hop(n, chain, step).wait_send()
                    self.across(n, chain, step, self.x).wait_send()


def solve(mine_ref, base):
    moment = {}

    def mom(e):
        if e not in moment:
            moment[e] = jnp.broadcast_to(mine_ref[extra_row(e) : extra_row(e) + 1, :], (8, 128))
        return moment[e]

    gram = {}
    for i in range(TERMS):
        for j in range(i, TERMS):
            value = None
            for factor, e in gram_terms(i, j):
                part = mom(e) if factor == 1.0 else factor * mom(e)
                value = part if value is None else value + part
            gram[i, j] = value
    cross = [mine_ref[pl.ds(k, 8, stride=8), :] for k in range(TERMS)]
    work = dict(gram)
    for i in range(TERMS):
        work[i, i] = work[i, i] + 1.0
    right = [cross[k] if base is None else cross[k] - base[k] for k in range(TERMS)]
    inverse, factor = [], {}
    for i in range(TERMS):
        inv = 1.0 / work[i, i]
        inverse.append(inv)
        for r in range(i + 1, TERMS):
            factor[r, i] = work[i, r] * inv
        for r in range(i + 1, TERMS):
            for c in range(r, TERMS):
                work[r, c] = work[r, c] - factor[r, i] * work[i, c]
            right[r] = right[r] - factor[r, i] * right[i]
    answer = [None] * TERMS
    for i in reversed(range(TERMS)):
        value = right[i] * inverse[i]
        for c in range(i + 1, TERMS):
            value = value - factor[c, i] * answer[c]
        answer[i] = value
    lost = None
    for i in range(TERMS):
        image = None
        for c in range(TERMS):
            part = gram[min(i, c), max(i, c)] * answer[c]
            image = part if image is None else image + part
        part = answer[i] * (2.0 * cross[i] - image)
        lost = part if lost is None else lost + part
    sub = lax.broadcasted_iota(jnp.int32, (8, 128), 0)
    lost = jnp.sum(jnp.where(sub < BANDS, lost, 0.0), axis=0, keepdims=True)
    spread = jnp.maximum(mom(EXTRA_S) - jnp.broadcast_to(lost, (8, 128)), 0.0) * (1.0 / BANDS)
    return answer, spread / (1.0 + mom(0))


def swap_halo(variance, own_ref, near_ref, sems):
    send, recv = sems
    s, j, x, z = place()
    own_ref[...] = variance
    copies = []
    for n, (a, b) in enumerate(NEIGHBOURS):
        back = NEIGHBOURS.index((-a, -b))
        copy = copy_to(
            own_ref, near_ref.at[back], send.at[n], recv.at[back], wrap(s + a, 16), wrap(j + b, SHARDS)
        )
        copy.start()
        copies.append(copy)
    return copies


def box_mean(variance, near_ref, copies):
    s, j, x, z = place()
    for copy in copies:
        copy.wait()
    lane = lax.broadcasted_iota(jnp.int32, (8, 128), 1)
    col, row = lane % 16, lane // 16

    def field(a, b):
        if (a, b) == (0, 0):
            return variance
        value = near_ref[NEIGHBOURS.index((a, b))]
        inside = jnp.int32(1)
        if a:
            inside = inside * ((s + a >= 0) & (s + a < 16)).astype(jnp.int32)
        if b:
            inside = inside * ((j + b >= 0) & (j + b < SHARDS)).astype(jnp.int32)
        return jnp.where(jnp.full((8, 128), inside) > 0, value, 0.0)

    across = []
    for a in (-1, 0, 1):
        middle = field(a, 0)
        left = pltpu.roll(field(a, -1), 128 - 16, 1)
        right = pltpu.roll(field(a, 1), 16, 1)
        total = middle
        for step in (1, 2):
            total = total + pltpu.roll(jnp.where(col < step, right, middle), 128 - step, 1)
            total = total + pltpu.roll(jnp.where(col >= 16 - step, left, middle), step, 1)
        across.append(total)
    up, middle, down = across
    total = middle
    for step in (1, 2):
        total = total + pltpu.roll(jnp.where(row < step, down, middle), 128 - 16 * step, 1)
        total = total + pltpu.roll(jnp.where(row >= 8 - step, up, middle), 16 * step, 1)

    def count(index, whole):
        return (jnp.minimum(index + 2, whole - 1) - jnp.maximum(index - 2, 0) + 1).astype(F32)

    return total / (count(s * 8 + row, 128) * count(j * 16 + col, COLS))


def whole(
    dates, days_ref, obs_hbm, valid_hbm, coef_ref, noise_ref,
    obs_ref, valid_ref, table_ref, w_ref, s_ref, r_ref, block_ref, in_sem, sp0, sp1, sp2, sp3, sp4, sp5, *rest,
):
    s, j, x, z = place()
    valid_copy = pltpu.make_async_copy(valid_hbm, valid_ref, in_sem.at[BANDS])
    valid_copy.start()
    obs_copies = [
        pltpu.make_async_copy(obs_hbm.at[b], obs_ref.at[b], in_sem.at[b]) for b in range(BANDS)
    ]
    for copy in obs_copies:
        copy.start()
    barrier, guests = greet()
    reductions, halos = [], []
    for n in range(2):
        mine_of = rest[18 * n : 18 * n + 18]
        mom, land = mine_of[:4], mine_of[4:8]
        slot, mine, own, near, xs, xr, rs, rr, hs, hr = mine_of[8:]
        reductions.append(Reduction(mom, land, slot, mine, (xs, xr, rs, rr)))
        halos.append((own, near, (hs, hr)))
    design_table(dates, days_ref, table_ref)
    valid_copy.wait()

    @pl.loop(0, dates)
    def _(d):
        w_ref[d] = valid_ref[d].astype(F32)

    red = reductions[0]

    def send_first(n):
        if n == 0:
            pl.semaphore_wait(barrier, guests)
        red.swap(n).start()

    form_moments(
        dates, lambda b, d, q: obs_ref[b, d, :, tile(q)].astype(F32), w_ref, table_ref, s_ref, red.mom,
        lambda b: obs_copies[b].wait(), send_first,
    )
    red.run()
    answer, variance = solve(red.mine, None)
    own_ref, near_ref, halo_sems = halos[0]
    copies = swap_halo(variance, own_ref, near_ref, halo_sems)
    base_row = pl.multiple_of(j * BLOCK, 8)
    for k in range(TERMS):
        block_ref[pl.ds(base_row + k, 8, stride=8), :] = answer[k]
    spread = Spread(block_ref, (sp0, sp1, sp2, sp3, sp4, sp5))
    spread.begin(0)
    spread.begin(1)
    smooth = box_mean(variance, near_ref, copies)
    block_ref[pl.ds(pl.multiple_of(base_row + 8 * BANDS, 8), 8), :] = smooth
    spread.begin(2)
    for step in range(1, 5):
        spread.relay(step)
    red.drain()
    spread.receive()
    form_residuals(dates, obs_ref, valid_ref, table_ref, block_ref, r_ref, w_ref)
    last = reductions[1]
    form_moments(
        dates, lambda b, d, q: r_ref[b, d, :, tile(q)], w_ref, table_ref, s_ref, last.mom,
        lambda b: None, lambda n: last.swap(n).start(),
    )
    spread.drain()
    last.run()
    base = [block_ref[pl.ds(base_row + k, 8, stride=8), :] for k in range(TERMS)]
    answer, variance = solve(last.mine, base)
    own_ref, near_ref, halo_sems = halos[1]
    copies = swap_halo(variance, own_ref, near_ref, halo_sems)
    masks = flip_masks()
    for k in range(TERMS):
        turned = flip(base[k] + answer[k], masks)
        for b in range(BANDS):
            coef_ref[b, k] = (turned if b == 0 else pltpu.roll(turned, 128 - 16 * b, 1))[:, :16]
    last.drain()
    smooth = box_mean(variance, near_ref, copies)
    noise_ref[...] = flip(jnp.sqrt(smooth + EPS), masks)[:, :16]


def reduction_scratch():
    pieces = len(PIECES)
    one, ring = pltpu.SemaphoreType.DMA((pieces,)), pltpu.SemaphoreType.DMA((4, 4, pieces))
    eight = pltpu.SemaphoreType.DMA((8,))
    return [
        *[pltpu.VMEM((SHARDS * count, 128), F32) for _, count in PIECES],
        *[pltpu.VMEM((ZS * count, 128), F32) for _, count in PIECES],
        pltpu.VMEM((4, 4, DEEP, 128), F32),
        pltpu.VMEM((DEEP, 128), F32),
        pltpu.VMEM((8, 128), F32),
        pltpu.VMEM((8, 8, 128), F32),
        one, one, ring, ring, eight, eight,
    ]


def on_device(obs, valid, days):
    dates = obs.shape[1]
    spread = pltpu.SemaphoreType.DMA((4, 4, len(PARTS)))
    own = pltpu.SemaphoreType.DMA((len(PARTS),))
    return pl.pallas_call(
        functools.partial(whole, dates),
        out_shape=(
            jax.ShapeDtypeStruct((BANDS, TERMS, ROWS, 16), F32),
            jax.ShapeDtypeStruct((ROWS, 16), F32),
        ),
        in_specs=[
            pl.BlockSpec(memory_space=pltpu.SMEM),
            pl.BlockSpec(memory_space=pl.ANY),
            pl.BlockSpec(memory_space=pl.ANY),
        ],
        out_specs=(pl.BlockSpec(memory_space=pltpu.VMEM), pl.BlockSpec(memory_space=pltpu.VMEM)),
        scratch_shapes=[
            pltpu.VMEM((BANDS, dates, ROWS, COLS), jnp.bfloat16),
            pltpu.VMEM((dates, ROWS, COLS), jnp.int32),
            pltpu.VMEM((dates * FIELDS, 128), F32),
            pltpu.VMEM((dates, ROWS, COLS), F32),
            pltpu.VMEM((ROWS, COLS), F32),
            pltpu.VMEM((BANDS, dates, ROWS, COLS), F32),
            pltpu.VMEM((SHARDS * BLOCK, 128), F32),
            pltpu.SemaphoreType.DMA((BANDS + 1,)),
            spread, spread, spread, spread, own, own,
            *reduction_scratch(),
            *reduction_scratch(),
        ],
        compiler_params=pltpu.CompilerParams(collective_id=0, has_side_effects=True, vmem_limit_bytes=56 << 20),
    )(days, obs, valid)


def solution(mesh):
    in_specs = (P(None, "date", "space", None), P("date", "space", None), P("date"))
    out_specs = (P(None, None, "space", "date"), P("space", "date"))
    return jax.shard_map(on_device, mesh=mesh, in_specs=in_specs, out_specs=out_specs, check_vma=False)
```

```python
import functools
import math

import jax
import jax.numpy as jnp
from jax import lax
from jax.experimental import pallas as pl
from jax.experimental.pallas import tpu as pltpu
from jax.sharding import PartitionSpec as P

F32 = jnp.float32
MESH = pl.DeviceIdType.MESH
TUKEY = 4.685
EPS = 1e-06
BANDS = 7
TERMS = 8
ROWS = 8
COLS = 512
WIDE = 256
TILES = 2
SHARDS = 32
DEEP = 80
BLOCK = 64
FIELDS = 24
ZS = 16
UNROLL = 4

C0, S0, TC0, TS0, EXTRA_S = 2, 8, 14, 17, 21
NEIGHBOURS = [(a, b) for a in (-1, 0, 1) for b in (-1, 0, 1) if (a, b) != (0, 0)]
PIECES = ((64, 16), (0, 24), (24, 24), (48, 16))
CHAINS = ((1, 8), (1, 7), (-1, 7), (-1, 6))
SPREADS = ((1, 2, 4), (1, 1, 4), (-1, 1, 4), (-1, 2, 3))
PARTS = ((0, 32), (32, 24), (56, 8))


def extra_row(e):
    return 64 + e if e < 16 else 40 + e


def gram_terms(i, j):
    if i > j:
        i, j = j, i
    if i == 0:
        if j < 2:
            return [(1.0, j)]
        n = j // 2
        return [(1.0, (C0 if j % 2 == 0 else S0) + n)]
    if i == 1:
        if j == 1:
            return [(1.0, 2)]
        n = j // 2
        return [(1.0, (TC0 if j % 2 == 0 else TS0) + n)]
    a, b = i // 2, j // 2

    def cosine(n):
        return 0 if n == 0 else C0 + n

    if i % 2 == 0 and j % 2 == 0:
        return [(0.5, cosine(abs(a - b))), (0.5, cosine(a + b))]
    if i % 2 == 1 and j % 2 == 1:
        return [(0.5, cosine(abs(a - b))), (-0.5, cosine(a + b))]
    s, c = (a, b) if i % 2 == 1 else (b, a)
    terms = [(0.5, S0 + s + c)]
    if s != c:
        terms.append((0.5 if s > c else -0.5, S0 + abs(s - c)))
    return terms


def turn(angle):
    turns = jnp.floor(angle * (0.5 / math.pi) + 0.5)
    half = 0.5 * ((angle - turns * 6.28125) - turns * (2.0 * math.pi - 6.28125))
    square = half * half
    s = jnp.full_like(half, 1.0 / math.factorial(13))
    for n in (11, 9, 7, 5, 3, 1):
        s = s * square + (1.0 if n % 4 == 1 else -1.0) / math.factorial(n)
    s = s * half
    c = jnp.full_like(half, 1.0 / math.factorial(12))
    for n in (10, 8, 6, 4, 2, 0):
        c = c * square + (1.0 if n % 4 == 0 else -1.0) / math.factorial(n)
    return 1.0 - 2.0 * s * s, 2.0 * s * c


def design_table(dates, first_date, day_ref, table_ref):
    day = day_ref[first_date : first_date + dates, :]
    t = (day - 1825.0) / 1825.0
    c1, s1 = turn(day * (2.0 * math.pi / 365.25))
    c, s = [None, c1, 1 - 2 * s1 * s1], [None, s1, 2 * s1 * c1]
    c.append(c1 * c[2] - s1 * s[2])
    s.append(s1 * c[2] + c1 * s[2])
    c += [1 - 2 * s[2] * s[2], c[2] * c[3] - s[2] * s[3], 1 - 2 * s[3] * s[3]]
    s += [2 * s[2] * c[2], s[2] * c[3] + c[2] * s[3], 2 * s[3] * c[3]]
    fields = [jnp.ones_like(t), t, t * t] + c[1:] + s[1:]
    fields += [t * c[h] for h in range(1, 4)] + [t * s[h] for h in range(1, 4)]
    for f, value in enumerate(fields):
        for first in range(0, dates, 8):
            start = (first_date + first) * FIELDS + f
            table_ref[pl.ds(start, 8, stride=FIELDS), :] = value[first : first + 8]


COLUMN = [0, 1, C0 + 1, S0 + 1, C0 + 2, S0 + 2, C0 + 3, S0 + 3]


def flip_masks():
    sub = lax.broadcasted_iota(jnp.int32, (8, 128), 0)
    group = lax.broadcasted_iota(jnp.int32, (8, 128), 1) // 16
    masks = []
    for bit in (4, 2, 1):
        s, g = (sub & bit) != 0, (group & bit) != 0
        masks.append((jnp.logical_and(s, jnp.logical_not(g)), jnp.logical_and(jnp.logical_not(s), g)))
    return masks


def flip(v, masks):
    for bit, (low, high) in zip((4, 2, 1), masks):
        up = pltpu.roll(pltpu.roll(v, bit, 0), 128 - 16 * bit, 1)
        if bit == 4:
            v = jnp.where(jnp.logical_or(low, high), up, v)
        else:
            down = pltpu.roll(pltpu.roll(v, 8 - bit, 0), 16 * bit, 1)
            v = jnp.where(low, up, jnp.where(high, down, v))
    return v


def tile(q):
    return slice(128 * q, 128 * q + 128)


def splat(table_ref, d, field):
    return table_ref[pl.ds(d * FIELDS + field, 8, stride=0), :]


def by_date(dates, one, carry):
    def body(n, carry):
        for u in range(UNROLL):
            carry = one(n * UNROLL + u, carry)
        return carry

    return lax.fori_loop(0, dates // UNROLL, body, carry)


def form_moments(dates, load, w_ref, table_ref, s_ref, out_refs, ready, done):
    masks = flip_masks()
    zero = jnp.zeros((8, 128), F32)

    def put(row, q, v):
        for (first, count), out_ref in zip(PIECES, out_refs):
            if first <= row < first + count:
                out_ref[pl.ds(q * 8 * count + row - first, 8, stride=count), :] = v

    for first in range(0, EXTRA_S, 11):
        fields = list(range(first, min(first + 11, EXTRA_S)))

        def one(d, acc):
            acc = list(acc)
            w = [w_ref[d, :, tile(q)] for q in range(TILES)]
            for n, e in enumerate(fields):
                x = splat(table_ref, d, e) if e else None
                for q in range(TILES):
                    acc[n * TILES + q] = acc[n * TILES + q] + (x * w[q] if e else w[q])
            return tuple(acc)

        acc = by_date(dates, one, (zero,) * (len(fields) * TILES))
        for n, e in enumerate(fields):
            for q in range(TILES):
                put(extra_row(e), q, flip(acc[n * TILES + q], masks))
    done(0)
    for b in range(BANDS):
        ready(b)

        def one(d, carry):
            acc, square = list(carry[0]), list(carry[1])
            wy = []
            for q in range(TILES):
                y = load(b, d, q)
                v = w_ref[d, :, tile(q)] * y
                square[q] = square[q] + v * y
                wy.append(v)
            for k in range(TERMS):
                x = splat(table_ref, d, COLUMN[k]) if k else None
                for q in range(TILES):
                    acc[k * TILES + q] = acc[k * TILES + q] + (x * wy[q] if k else wy[q])
            return tuple(acc), tuple(square)

        acc, square = by_date(dates, one, ((zero,) * (TERMS * TILES), (zero,) * TILES))
        for k in range(TERMS):
            for q in range(TILES):
                put(8 * b + k, q, flip(acc[k * TILES + q], masks))
        for q in range(TILES):
            total = square[q] if b == 0 else s_ref[:, tile(q)] + square[q]
            if b < BANDS - 1:
                s_ref[:, tile(q)] = total
            else:
                put(extra_row(EXTRA_S), q, flip(total, masks))
                for row in range(extra_row(EXTRA_S) + 1, 64):
                    put(row, q, zero)
        for n, (first, count) in enumerate(PIECES):
            if n and 8 * b + 8 == min(first + count, 8 * BANDS):
                done(n)


def form_residuals(dates, obs_ref, mask_ref, table_ref, block_ref, r_ref, w_ref):
    masks = flip_masks()

    def get(row, q):
        return flip(block_ref[pl.ds(q * 8 * BLOCK + row, 8, stride=BLOCK), :], masks)

    for b in range(BANDS):
        beta = [[get(8 * b + k, q) for q in range(TILES)] for k in range(TERMS)]

        def one(d, carry):
            x = [splat(table_ref, d, COLUMN[k]) if k else None for k in range(TERMS)]
            for q in range(TILES):
                fit = beta[0][q]
                for k in range(1, TERMS):
                    fit = fit + x[k] * beta[k][q]
                r = obs_ref[b, d, :, tile(q)].astype(F32) - fit
                r_ref[b, d, :, tile(q)] = r
                if b == 0:
                    w_ref[d, :, tile(q)] = r * r
                else:
                    w_ref[d, :, tile(q)] = w_ref[d, :, tile(q)] + r * r
            return carry

        by_date(dates, one, 0)
    scale = [1.0 / (float(BANDS) * (TUKEY * TUKEY) * (get(8 * BANDS, q) + EPS)) for q in range(TILES)]

    def weigh(d, carry):
        for q in range(TILES):
            left = 1.0 - jnp.minimum(w_ref[d, :, tile(q)] * scale[q], 1.0)
            w_ref[d, :, tile(q)] = mask_ref[d, :, tile(q)] * left * left
        return carry

    by_date(dates, weigh, 0)


def copy_to(src, dst, send, recv, space, date):
    return pltpu.make_async_remote_copy(
        src_ref=src, dst_ref=dst, send_sem=send, recv_sem=recv, device_id=(space, date), device_id_type=MESH
    )


def place():
    s, j = lax.axis_index("space"), lax.axis_index("date")
    return s, j, j // ZS, lax.rem(j, ZS)


def wrap(value, count):
    return lax.rem(value + count, count)


def greet():
    s, j, x, z = place()
    sem = pltpu.get_barrier_semaphore()
    targets = [(s, x * ZS + wrap(z + h, ZS)) for h in (1, -1, 2, -2)] + [(s, (1 - x) * ZS + z)]
    targets += [(wrap(s + a, 16), wrap(j + b, SHARDS)) for a, b in NEIGHBOURS]
    for target in targets:
        pl.semaphore_signal(sem, inc=1, device_id=target, device_id_type=MESH)
    return sem, len(targets)


class Reduction:
    def __init__(self, mom_refs, slot_ref, mine_ref, sems):
        self.mom, self.slot, self.mine = mom_refs, slot_ref, mine_ref
        self.send, self.recv = sems
        self.s, self.j, self.x, self.z = place()

    def length(self, chain):
        return (CHAINS[chain][1] + 1) // 2

    def rows(self, n, chain, step):
        way, first = CHAINS[chain]
        count = PIECES[n][1]
        return pl.ds(pl.multiple_of(wrap(self.z + way * (first - 2 * step), ZS) * count, 8), count)

    def place_of(self, n, chain, step):
        return self.slot.at[chain, step, pl.ds(*PIECES[n])]

    def hop(self, n, chain, step):
        way, first = CHAINS[chain]
        reach = min(2, first - 2 * step)
        source = self.mom[n].at[self.rows(n, chain, 0)] if step == 0 else self.place_of(n, chain, step - 1)
        return copy_to(
            source, self.place_of(n, chain, step), self.send.at[chain, step, n], self.recv.at[chain, step, n],
            self.s, self.x * ZS + wrap(self.z + way * reach, ZS),
        )

    def step(self, n, step):
        for chain in range(4):
            if step >= self.length(chain):
                continue
            if step:
                self.hop(n, chain, step - 1).wait_recv()
                here = self.place_of(n, chain, step - 1)
                here[...] = here[...] + self.mom[n][self.rows(n, chain, step), :]
            self.hop(n, chain, step).start()

    def finish(self, n):
        first, count = PIECES[n]
        total = self.mom[n][pl.ds(pl.multiple_of(self.z * count, 8), count), :]
        for chain in range(4):
            last = self.length(chain) - 1
            self.hop(n, chain, last).wait_recv()
            total = total + self.slot[chain, last, pl.ds(first, count), :]
        self.mine[pl.ds(first, count), :] = total

    def wave(self, wave):
        for n in range(len(PIECES)):
            if 0 <= wave - n < 4:
                self.step(n, wave - n)
            if wave - n == 4:
                self.finish(n)

    def run(self):
        for wave in range(len(PIECES), len(PIECES) + 4):
            self.wave(wave)

    def drain(self):
        for n in range(len(PIECES)):
            for chain in range(4):
                for step in range(self.length(chain)):
                    self.hop(n, chain, step).wait_send()


class Spread:
    def __init__(self, block_ref, sems):
        self.block = block_ref
        self.send, self.recv = sems
        self.s, self.j, self.x, self.z = place()

    def piece(self, owner, n):
        first, count = PARTS[n]
        return self.block.at[pl.ds(pl.multiple_of(wrap(owner + ZS, ZS) * BLOCK + first, 8), count)]

    def offset(self, chain, step):
        way, first, _ = SPREADS[chain]
        return 0 if step == 0 else way * (first + 2 * (step - 1))

    def hop(self, n, chain, step):
        way, first, _ = SPREADS[chain]
        reach = first if step == 0 else 2
        piece = self.piece(self.z - self.offset(chain, step), n)
        return copy_to(
            piece, piece, self.send.at[chain, step, n], self.recv.at[chain, step, n],
            self.s, self.x * ZS + wrap(self.z + way * reach, ZS),
        )

    def arrival(self, n, chain, step):
        piece = self.piece(self.z - self.offset(chain, step + 1), n)
        return copy_to(
            piece, piece, self.send.at[chain, step, n], self.recv.at[chain, step, n], self.s, self.j
        )

    def begin(self, n):
        for chain in range(4):
            self.hop(n, chain, 0).start()

    def relay(self, step):
        for n in range(len(PARTS)):
            for chain in range(4):
                if step <= SPREADS[chain][2]:
                    self.arrival(n, chain, step - 1).wait_recv()
                    if step < SPREADS[chain][2]:
                        self.hop(n, chain, step).start()

    def drain(self):
        for n in range(len(PARTS)):
            for chain in range(4):
                for step in range(SPREADS[chain][2]):
                    self.hop(n, chain, step).wait_send()


def solve(mine_ref, base):
    moment = {}

    def mom(e):
        if e not in moment:
            moment[e] = jnp.broadcast_to(mine_ref[extra_row(e) : extra_row(e) + 1, :], (8, 128))
        return moment[e]

    gram = {}
    for i in range(TERMS):
        for j in range(i, TERMS):
            value = None
            for factor, e in gram_terms(i, j):
                part = mom(e) if factor == 1.0 else factor * mom(e)
                value = part if value is None else value + part
            gram[i, j] = value
    cross = [mine_ref[pl.ds(k, 8, stride=8), :] for k in range(TERMS)]
    work = dict(gram)
    for i in range(TERMS):
        work[i, i] = work[i, i] + 1.0
    right = [cross[k] if base is None else cross[k] - base[k] for k in range(TERMS)]
    inverse, factor = [], {}
    for i in range(TERMS):
        inv = 1.0 / work[i, i]
        inverse.append(inv)
        for r in range(i + 1, TERMS):
            factor[r, i] = work[i, r] * inv
        for r in range(i + 1, TERMS):
            for c in range(r, TERMS):
                work[r, c] = work[r, c] - factor[r, i] * work[i, c]
            right[r] = right[r] - factor[r, i] * right[i]
    answer = [None] * TERMS
    for i in reversed(range(TERMS)):
        value = right[i] * inverse[i]
        for c in range(i + 1, TERMS):
            value = value - factor[c, i] * answer[c]
        answer[i] = value
    lost = None
    for i in range(TERMS):
        image = None
        for c in range(TERMS):
            part = gram[min(i, c), max(i, c)] * answer[c]
            image = part if image is None else image + part
        part = answer[i] * (2.0 * cross[i] - image)
        lost = part if lost is None else lost + part
    sub = lax.broadcasted_iota(jnp.int32, (8, 128), 0)
    lost = jnp.sum(jnp.where(sub < BANDS, lost, 0.0), axis=0, keepdims=True)
    spread = jnp.maximum(mom(EXTRA_S) - jnp.broadcast_to(lost, (8, 128)), 0.0) * (1.0 / BANDS)
    return answer, spread / (1.0 + mom(0))


def swap_halo(variance, own_ref, near_ref, sems):
    send, recv = sems
    s, j, x, z = place()
    own_ref[...] = variance
    copies = []
    for n, (a, b) in enumerate(NEIGHBOURS):
        back = NEIGHBOURS.index((-a, -b))
        copy = copy_to(
            own_ref, near_ref.at[back], send.at[n], recv.at[back], wrap(s + a, 16), wrap(j + b, SHARDS)
        )
        copy.start()
        copies.append(copy)
    return copies


def box_mean(variance, near_ref, copies):
    s, j, x, z = place()
    for copy in copies:
        copy.wait()
    lane = lax.broadcasted_iota(jnp.int32, (8, 128), 1)
    col, row = lane % 16, lane // 16

    def field(a, b):
        if (a, b) == (0, 0):
            return variance
        value = near_ref[NEIGHBOURS.index((a, b))]
        inside = jnp.int32(1)
        if a:
            inside = inside * ((s + a >= 0) & (s + a < 16)).astype(jnp.int32)
        if b:
            inside = inside * ((j + b >= 0) & (j + b < SHARDS)).astype(jnp.int32)
        return jnp.where(jnp.full((8, 128), inside) > 0, value, 0.0)

    across = []
    for a in (-1, 0, 1):
        middle = field(a, 0)
        left = pltpu.roll(field(a, -1), 128 - 16, 1)
        right = pltpu.roll(field(a, 1), 16, 1)
        total = middle
        for step in (1, 2):
            total = total + pltpu.roll(jnp.where(col < step, right, middle), 128 - step, 1)
            total = total + pltpu.roll(jnp.where(col >= 16 - step, left, middle), step, 1)
        across.append(total)
    up, middle, down = across
    total = middle
    for step in (1, 2):
        total = total + pltpu.roll(jnp.where(row < step, down, middle), 128 - 16 * step, 1)
        total = total + pltpu.roll(jnp.where(row >= 8 - step, up, middle), 16 * step, 1)

    def count(index, whole):
        return (jnp.minimum(index + 2, whole - 1) - jnp.maximum(index - 2, 0) + 1).astype(F32)

    return total / (count(s * 8 + row, 128) * count(j * 16 + col, COLS))


def whole(
    dates, days_ref, obs_hbm, valid_hbm, out_ref,
    obs_ref, valid_ref, turned_ref, day_ref, table_ref, mask_ref, w_ref, s_ref, r_ref, block_ref,
    in_sem, trade_send, trade_recv, sp_send, sp_recv, *rest,
):
    s, j, x, z = place()
    own = pl.ds(pl.multiple_of(x * WIDE, 128), WIDE)
    other = pl.ds(pl.multiple_of((1 - x) * WIDE, 128), WIDE)
    early, late = pl.ds(0, dates), pl.ds(dates, dates)
    valid_copies = [
        pltpu.make_async_copy(valid_hbm.at[:, :, cols], valid_ref.at[n], in_sem.at[BANDS + n])
        for n, cols in ((1, other), (0, own))
    ]
    obs_copies = [
        pltpu.make_async_copy(obs_hbm.at[b, :, :, own], obs_ref.at[b, early], in_sem.at[b]) for b in range(BANDS)
    ]
    for copy in valid_copies + obs_copies:
        copy.start()
    barrier, guests = greet()
    partner = (s, (1 - x) * ZS + z)

    def trade(n, src, dst):
        return copy_to(src, dst, trade_send.at[n], trade_recv.at[n], *partner)

    trades = [
        trade(b, obs_hbm.at[b, :, :, other], obs_ref.at[b, late]) for b in range(BANDS)
    ]
    day_trade = trade(BANDS, day_ref.at[early], day_ref.at[late])
    mask_trade = trade(BANDS + 1, turned_ref.at[0], turned_ref.at[1])
    rows = lax.broadcasted_iota(jnp.int32, (dates, 128), 0)
    day = jnp.zeros((dates, 128), F32)
    for d in range(dates):
        day = jnp.where(rows == d, days_ref[d].astype(F32), day)
    day_ref[0:dates, :] = day
    valid_copies[0].wait()

    @pl.loop(0, dates)
    def _(d):
        turned_ref[0, d] = valid_ref[1, d].astype(F32).astype(jnp.bfloat16)

    design_table(dates, 0, day_ref, table_ref)
    pl.semaphore_wait(barrier, guests)
    day_trade.start()
    mask_trade.start()
    for copy in trades:
        copy.start()
    valid_copies[1].wait()

    @pl.loop(0, dates)
    def _(d):
        mask_ref[d] = valid_ref[0, d].astype(F32)

    day_trade.wait_recv()
    design_table(dates, dates, day_ref, table_ref)
    mask_trade.wait_recv()

    @pl.loop(0, dates)
    def _(d):
        mask_ref[dates + d] = turned_ref[1, d].astype(F32)

    reductions, halos = [], []
    for n in range(2):
        part = rest[12 * n : 12 * n + 12]
        reductions.append(Reduction(part[:4], part[4], part[5], part[8:10]))
        halos.append((part[6], part[7], part[10:12]))

    def ready(b):
        obs_copies[b].wait()
        trades[b].wait_recv()

    both = 2 * dates
    first, last = reductions
    form_moments(
        both, lambda b, d, q: obs_ref[b, d, :, tile(q)].astype(F32), mask_ref, table_ref, s_ref, first.mom,
        ready, first.wave,
    )
    first.run()
    answer, variance = solve(first.mine, None)
    own_ref, near_ref, halo_sems = halos[0]
    copies = swap_halo(variance, own_ref, near_ref, halo_sems)
    base_row = pl.multiple_of(z * BLOCK, 8)
    for k in range(TERMS):
        block_ref[pl.ds(base_row + k, 8, stride=8), :] = answer[k]
    spread = Spread(block_ref, (sp_send, sp_recv))
    spread.begin(0)
    spread.begin(1)
    smooth = box_mean(variance, near_ref, copies)
    block_ref[pl.ds(pl.multiple_of(base_row + 8 * BANDS, 8), 8), :] = smooth
    spread.begin(2)
    for step in range(1, 5):
        spread.relay(step)
    form_residuals(both, obs_ref, mask_ref, table_ref, block_ref, r_ref, w_ref)
    form_moments(
        both, lambda b, d, q: r_ref[b, d, :, tile(q)], w_ref, table_ref, s_ref, last.mom,
        lambda b: None, last.wave,
    )
    spread.drain()
    first.drain()
    for copy in trades + [day_trade, mask_trade]:
        copy.wait_send()
    last.run()
    base = [block_ref[pl.ds(base_row + k, 8, stride=8), :] for k in range(TERMS)]
    answer, variance = solve(last.mine, base)
    own_ref, near_ref, halo_sems = halos[1]
    copies = swap_halo(variance, own_ref, near_ref, halo_sems)
    masks = flip_masks()
    for k in range(TERMS):
        turned = flip(base[k] + answer[k], masks)
        for b in range(BANDS):
            out_ref[b * TERMS + k] = (turned if b == 0 else pltpu.roll(turned, 128 - 16 * b, 1))[:, :16]
    last.drain()
    smooth = box_mean(variance, near_ref, copies)
    out_ref[BANDS * TERMS] = flip(jnp.sqrt(smooth + EPS), masks)[:, :16]


def reduction_scratch():
    ring, eight = pltpu.SemaphoreType.DMA((4, 4, len(PIECES))), pltpu.SemaphoreType.DMA((8,))
    return [
        *[pltpu.VMEM((ZS * count, 128), F32) for _, count in PIECES],
        pltpu.VMEM((4, 4, DEEP, 128), F32),
        pltpu.VMEM((DEEP, 128), F32),
        pltpu.VMEM((8, 128), F32),
        pltpu.VMEM((8, 8, 128), F32),
        ring, ring, eight, eight,
    ]


def on_device(obs, valid, days):
    dates = obs.shape[1]
    spread = pltpu.SemaphoreType.DMA((4, 4, len(PARTS)))
    trade = pltpu.SemaphoreType.DMA((BANDS + 2,))
    out = pl.pallas_call(
        functools.partial(whole, dates),
        out_shape=jax.ShapeDtypeStruct((BANDS * TERMS + 1, ROWS, 16), F32),
        in_specs=[
            pl.BlockSpec(memory_space=pltpu.SMEM),
            pl.BlockSpec(memory_space=pl.ANY),
            pl.BlockSpec(memory_space=pl.ANY),
        ],
        out_specs=pl.BlockSpec(memory_space=pltpu.VMEM),
        scratch_shapes=[
            pltpu.VMEM((BANDS, 2 * dates, ROWS, WIDE), jnp.bfloat16),
            pltpu.VMEM((2, dates, ROWS, WIDE), jnp.int32),
            pltpu.VMEM((2, dates, ROWS, WIDE), jnp.bfloat16),
            pltpu.VMEM((2 * dates, 128), F32),
            pltpu.VMEM((2 * dates * FIELDS, 128), F32),
            pltpu.VMEM((2 * dates, ROWS, WIDE), F32),
            pltpu.VMEM((2 * dates, ROWS, WIDE), F32),
            pltpu.VMEM((ROWS, WIDE), F32),
            pltpu.VMEM((BANDS, 2 * dates, ROWS, WIDE), F32),
            pltpu.VMEM((ZS * BLOCK, 128), F32),
            pltpu.SemaphoreType.DMA((BANDS + 2,)),
            trade, trade, spread, spread,
            *reduction_scratch(),
            *reduction_scratch(),
        ],
        compiler_params=pltpu.CompilerParams(collective_id=0, has_side_effects=True, vmem_limit_bytes=56 << 20),
    )(days, obs, valid)
    return out[: BANDS * TERMS].reshape(BANDS, TERMS, ROWS, 16), out[BANDS * TERMS]


def solution(mesh):
    in_specs = (P(None, "date", "space", None), P("date", "space", None), P("date"))
    out_specs = (P(None, None, "space", "date"), P("space", "date"))
    return jax.shard_map(on_device, mesh=mesh, in_specs=in_specs, out_specs=out_specs, check_vma=False)
```

```python
import functools
import math

import jax
import jax.numpy as jnp
from jax import lax
from jax.experimental import pallas as pl
from jax.experimental.pallas import tpu as pltpu
from jax.sharding import PartitionSpec as P

F32 = jnp.float32
MESH = pl.DeviceIdType.MESH
TUKEY = 4.685
EPS = 1e-06
BANDS = 7
TERMS = 8
ROWS = 8
COLS = 512
WIDE = 256
TILES = 2
SHARDS = 32
DEEP = 80
BLOCK = 64
FIELDS = 24
ZS = 16
UNROLL = 4

C0, S0, TC0, TS0, EXTRA_S = 2, 8, 14, 17, 21
NEIGHBOURS = [(a, b) for a in (-1, 0, 1) for b in (-1, 0, 1) if (a, b) != (0, 0)]
PIECES = ((64, 16), (0, 16), (16, 24), (40, 24))
BY_TWO = ((1, 8, 2), (1, 7, 2), (-1, 7, 2), (-1, 6, 2))
BY_FOUR = tuple((1, n, 4) for n in (8, 7, 6, 5)) + tuple((-1, n, 4) for n in (7, 6, 5, 4))
CHAINS = (BY_TWO, BY_TWO, BY_TWO, BY_FOUR)
SLOW_PLAN = (
    ((0, 0),),
    ((1, 0), (0, 1)),
    ((2, 0), (1, 1), (0, 2)),
    ((3, 0),),
    ((0, 3), (1, 2), (2, 1), (0, 4), (1, 3), (2, 2), (3, 1), (1, 4), (2, 3), (3, 2), (2, 4)),
)
FAST_PLAN = (
    ((0, 0),),
    ((1, 0),),
    ((2, 0),),
    ((3, 0),),
    ((0, 1), (1, 1), (2, 1), (0, 2), (1, 2), (3, 1), (2, 2), (0, 3), (1, 3), (2, 3), (0, 4), (1, 4), (3, 2), (2, 4)),
)
OUT_BY_TWO = ((1, 2, 4, 2), (1, 1, 4, 2), (-1, 1, 4, 2), (-1, 2, 3, 2))
OUT_BY_FOUR = tuple((1, n, 2, 4) for n in (4, 3, 2, 1)) + tuple((-1, n, 2 if n < 4 else 1, 4) for n in (4, 3, 2, 1))
SPREADS = (OUT_BY_TWO, OUT_BY_TWO, OUT_BY_FOUR)
PARTS = ((0, 32), (32, 24), (56, 8))


def extra_row(e):
    return 64 + e if e < 16 else 40 + e


def gram_terms(i, j):
    if i > j:
        i, j = j, i
    if i == 0:
        if j < 2:
            return [(1.0, j)]
        n = j // 2
        return [(1.0, (C0 if j % 2 == 0 else S0) + n)]
    if i == 1:
        if j == 1:
            return [(1.0, 2)]
        n = j // 2
        return [(1.0, (TC0 if j % 2 == 0 else TS0) + n)]
    a, b = i // 2, j // 2

    def cosine(n):
        return 0 if n == 0 else C0 + n

    if i % 2 == 0 and j % 2 == 0:
        return [(0.5, cosine(abs(a - b))), (0.5, cosine(a + b))]
    if i % 2 == 1 and j % 2 == 1:
        return [(0.5, cosine(abs(a - b))), (-0.5, cosine(a + b))]
    s, c = (a, b) if i % 2 == 1 else (b, a)
    terms = [(0.5, S0 + s + c)]
    if s != c:
        terms.append((0.5 if s > c else -0.5, S0 + abs(s - c)))
    return terms


def turn(angle):
    turns = jnp.floor(angle * (0.5 / math.pi) + 0.5)
    half = 0.5 * ((angle - turns * 6.28125) - turns * (2.0 * math.pi - 6.28125))
    square = half * half
    s = jnp.full_like(half, 1.0 / math.factorial(13))
    for n in (11, 9, 7, 5, 3, 1):
        s = s * square + (1.0 if n % 4 == 1 else -1.0) / math.factorial(n)
    s = s * half
    c = jnp.full_like(half, 1.0 / math.factorial(12))
    for n in (10, 8, 6, 4, 2, 0):
        c = c * square + (1.0 if n % 4 == 0 else -1.0) / math.factorial(n)
    return 1.0 - 2.0 * s * s, 2.0 * s * c


def design_table(dates, first_date, day_ref, table_ref):
    day = day_ref[first_date : first_date + dates, :]
    t = (day - 1825.0) / 1825.0
    c1, s1 = turn(day * (2.0 * math.pi / 365.25))
    c, s = [None, c1, 1 - 2 * s1 * s1], [None, s1, 2 * s1 * c1]
    c.append(c1 * c[2] - s1 * s[2])
    s.append(s1 * c[2] + c1 * s[2])
    c += [1 - 2 * s[2] * s[2], c[2] * c[3] - s[2] * s[3], 1 - 2 * s[3] * s[3]]
    s += [2 * s[2] * c[2], s[2] * c[3] + c[2] * s[3], 2 * s[3] * c[3]]
    fields = [jnp.ones_like(t), t, t * t] + c[1:] + s[1:]
    fields += [t * c[h] for h in range(1, 4)] + [t * s[h] for h in range(1, 4)]
    for f, value in enumerate(fields):
        for first in range(0, dates, 8):
            start = (first_date + first) * FIELDS + f
            table_ref[pl.ds(start, 8, stride=FIELDS), :] = value[first : first + 8]


COLUMN = [0, 1, C0 + 1, S0 + 1, C0 + 2, S0 + 2, C0 + 3, S0 + 3]


def flip_masks():
    sub = lax.broadcasted_iota(jnp.int32, (8, 128), 0)
    group = lax.broadcasted_iota(jnp.int32, (8, 128), 1) // 16
    masks = []
    for bit in (4, 2, 1):
        s, g = (sub & bit) != 0, (group & bit) != 0
        masks.append((jnp.logical_and(s, jnp.logical_not(g)), jnp.logical_and(jnp.logical_not(s), g)))
    return masks


def flip(v, masks):
    for bit, (low, high) in zip((4, 2, 1), masks):
        up = pltpu.roll(pltpu.roll(v, bit, 0), 128 - 16 * bit, 1)
        if bit == 4:
            v = jnp.where(jnp.logical_or(low, high), up, v)
        else:
            down = pltpu.roll(pltpu.roll(v, 8 - bit, 0), 16 * bit, 1)
            v = jnp.where(low, up, jnp.where(high, down, v))
    return v


def tile(q):
    return slice(128 * q, 128 * q + 128)


def splat(table_ref, d, field):
    return table_ref[pl.ds(d * FIELDS + field, 8, stride=0), :]


def by_date(dates, one, carry):
    def body(n, carry):
        for u in range(UNROLL):
            carry = one(n * UNROLL + u, carry)
        return carry

    return lax.fori_loop(0, dates // UNROLL, body, carry)


def form_moments(dates, load, w_ref, table_ref, s_ref, out_refs, ready, done):
    masks = flip_masks()
    zero = jnp.zeros((8, 128), F32)

    def put(row, q, v):
        for (first, count), out_ref in zip(PIECES, out_refs):
            if first <= row < first + count:
                out_ref[pl.ds(q * 8 * count + row - first, 8, stride=count), :] = v

    for first in range(0, EXTRA_S, 11):
        fields = list(range(first, min(first + 11, EXTRA_S)))

        def one(d, acc):
            acc = list(acc)
            w = [w_ref[d, :, tile(q)] for q in range(TILES)]
            for n, e in enumerate(fields):
                x = splat(table_ref, d, e) if e else None
                for q in range(TILES):
                    acc[n * TILES + q] = acc[n * TILES + q] + (x * w[q] if e else w[q])
            return tuple(acc)

        acc = by_date(dates, one, (zero,) * (len(fields) * TILES))
        for n, e in enumerate(fields):
            for q in range(TILES):
                put(extra_row(e), q, flip(acc[n * TILES + q], masks))
    done(0)
    for b in range(BANDS):
        ready(b)

        def one(d, carry):
            acc, square = list(carry[0]), list(carry[1])
            wy = []
            for q in range(TILES):
                y = load(b, d, q)
                v = w_ref[d, :, tile(q)] * y
                square[q] = square[q] + v * y
                wy.append(v)
            for k in range(TERMS):
                x = splat(table_ref, d, COLUMN[k]) if k else None
                for q in range(TILES):
                    acc[k * TILES + q] = acc[k * TILES + q] + (x * wy[q] if k else wy[q])
            return tuple(acc), tuple(square)

        acc, square = by_date(dates, one, ((zero,) * (TERMS * TILES), (zero,) * TILES))
        for k in range(TERMS):
            for q in range(TILES):
                put(8 * b + k, q, flip(acc[k * TILES + q], masks))
        for q in range(TILES):
            total = square[q] if b == 0 else s_ref[:, tile(q)] + square[q]
            if b < BANDS - 1:
                s_ref[:, tile(q)] = total
            else:
                put(extra_row(EXTRA_S), q, flip(total, masks))
                for row in range(extra_row(EXTRA_S) + 1, 64):
                    put(row, q, zero)
        for n, (first, count) in enumerate(PIECES):
            if n and 8 * b + 8 == min(first + count, 8 * BANDS):
                done(n)


def form_residuals(dates, obs_ref, mask_ref, table_ref, block_ref, r_ref, w_ref, smooth_ready):
    masks = flip_masks()

    def get(row, q):
        return flip(block_ref[pl.ds(q * 8 * BLOCK + row, 8, stride=BLOCK), :], masks)

    for b in range(BANDS):
        beta = [[get(8 * b + k, q) for q in range(TILES)] for k in range(TERMS)]

        def one(d, carry):
            x = [splat(table_ref, d, COLUMN[k]) if k else None for k in range(TERMS)]
            for q in range(TILES):
                fit = beta[0][q]
                for k in range(1, TERMS):
                    fit = fit + x[k] * beta[k][q]
                r = obs_ref[b, d, :, tile(q)].astype(F32) - fit
                r_ref[b, d, :, tile(q)] = r
                if b == 0:
                    w_ref[d, :, tile(q)] = r * r
                else:
                    w_ref[d, :, tile(q)] = w_ref[d, :, tile(q)] + r * r
            return carry

        by_date(dates, one, 0)
    smooth_ready()
    scale = [1.0 / (float(BANDS) * (TUKEY * TUKEY) * (get(8 * BANDS, q) + EPS)) for q in range(TILES)]

    def weigh(d, carry):
        for q in range(TILES):
            left = 1.0 - jnp.minimum(w_ref[d, :, tile(q)] * scale[q], 1.0)
            w_ref[d, :, tile(q)] = mask_ref[d, :, tile(q)] * left * left
        return carry

    by_date(dates, weigh, 0)


def copy_to(src, dst, send, recv, space, date):
    return pltpu.make_async_remote_copy(
        src_ref=src, dst_ref=dst, send_sem=send, recv_sem=recv, device_id=(space, date), device_id_type=MESH
    )


def place():
    s, j = lax.axis_index("space"), lax.axis_index("date")
    return s, j, j // ZS, lax.rem(j, ZS)


def wrap(value, count):
    return lax.rem(value + count, count)


def greet():
    s, j, x, z = place()
    sem = pltpu.get_barrier_semaphore()
    targets = [(s, x * ZS + wrap(z + h, ZS)) for h in (1, -1, 2, -2, 3, -3, 4, -4)] + [(s, (1 - x) * ZS + z)]
    targets += [(wrap(s + a, 16), wrap(j + b, SHARDS)) for a, b in NEIGHBOURS]
    for target in targets:
        pl.semaphore_signal(sem, inc=1, device_id=target, device_id_type=MESH)
    return sem, len(targets)


class Reduction:
    def __init__(self, mom_refs, slot_ref, mine_ref, sems, plan):
        self.mom, self.slot, self.mine, self.plan = mom_refs, slot_ref, mine_ref, plan
        self.send, self.recv = sems
        self.s, self.j, self.x, self.z = place()

    def length(self, n, chain):
        _, first, stride = CHAINS[n][chain]
        return (first + stride - 1) // stride

    def rows(self, n, chain, step):
        way, first, stride = CHAINS[n][chain]
        count = PIECES[n][1]
        return pl.ds(pl.multiple_of(wrap(self.z + way * (first - stride * step), ZS) * count, 8), count)

    def place_of(self, n, chain, step):
        return self.slot.at[chain, step, pl.ds(*PIECES[n])]

    def hop(self, n, chain, step):
        way, first, stride = CHAINS[n][chain]
        reach = min(stride, first - stride * step)
        source = self.mom[n].at[self.rows(n, chain, 0)] if step == 0 else self.place_of(n, chain, step - 1)
        return copy_to(
            source, self.place_of(n, chain, step), self.send.at[chain, step, n], self.recv.at[chain, step, n],
            self.s, self.x * ZS + wrap(self.z + way * reach, ZS),
        )

    def step(self, n, step):
        for chain in range(len(CHAINS[n])):
            if step >= self.length(n, chain):
                continue
            if step:
                self.hop(n, chain, step - 1).wait_recv()
                here = self.place_of(n, chain, step - 1)
                here[...] = here[...] + self.mom[n][self.rows(n, chain, step), :]
            self.hop(n, chain, step).start()

    def finish(self, n):
        first, count = PIECES[n]
        total = self.mom[n][pl.ds(pl.multiple_of(self.z * count, 8), count), :]
        for chain in range(len(CHAINS[n])):
            last = self.length(n, chain) - 1
            self.hop(n, chain, last).wait_recv()
            total = total + self.slot[chain, last, pl.ds(first, count), :]
        self.mine[pl.ds(first, count), :] = total

    def advance(self, stage):
        for n, step in self.plan[stage]:
            if step == max(self.length(n, chain) for chain in range(len(CHAINS[n]))):
                self.finish(n)
            else:
                self.step(n, step)

    def run(self):
        self.advance(len(PIECES))

    def drain(self):
        for n in range(len(PIECES)):
            for chain in range(len(CHAINS[n])):
                for step in range(self.length(n, chain)):
                    self.hop(n, chain, step).wait_send()


class Spread:
    def __init__(self, block_ref, sems):
        self.block = block_ref
        self.send, self.recv = sems
        self.s, self.j, self.x, self.z = place()

    def piece(self, owner, n):
        first, count = PARTS[n]
        return self.block.at[pl.ds(pl.multiple_of(wrap(owner + ZS, ZS) * BLOCK + first, 8), count)]

    def offset(self, n, chain, step):
        way, first, _, stride = SPREADS[n][chain]
        return 0 if step == 0 else way * (first + stride * (step - 1))

    def hop(self, n, chain, step):
        way, first, _, stride = SPREADS[n][chain]
        reach = first if step == 0 else stride
        piece = self.piece(self.z - self.offset(n, chain, step), n)
        return copy_to(
            piece, piece, self.send.at[chain, step, n], self.recv.at[chain, step, n],
            self.s, self.x * ZS + wrap(self.z + way * reach, ZS),
        )

    def arrival(self, n, chain, step):
        piece = self.piece(self.z - self.offset(n, chain, step + 1), n)
        return copy_to(
            piece, piece, self.send.at[chain, step, n], self.recv.at[chain, step, n], self.s, self.j
        )

    def begin(self, n):
        for chain in range(len(SPREADS[n])):
            self.hop(n, chain, 0).start()

    def relay(self, n, step):
        for chain in range(len(SPREADS[n])):
            if step <= SPREADS[n][chain][2]:
                self.arrival(n, chain, step - 1).wait_recv()
                if step < SPREADS[n][chain][2]:
                    self.hop(n, chain, step).start()

    def drain(self):
        for n in range(len(PARTS)):
            for chain in range(len(SPREADS[n])):
                for step in range(SPREADS[n][chain][2]):
                    self.hop(n, chain, step).wait_send()


def solve(mine_ref, base):
    moment = {}

    def mom(e):
        if e not in moment:
            moment[e] = jnp.broadcast_to(mine_ref[extra_row(e) : extra_row(e) + 1, :], (8, 128))
        return moment[e]

    gram = {}
    for i in range(TERMS):
        for j in range(i, TERMS):
            value = None
            for factor, e in gram_terms(i, j):
                part = mom(e) if factor == 1.0 else factor * mom(e)
                value = part if value is None else value + part
            gram[i, j] = value
    cross = [mine_ref[pl.ds(k, 8, stride=8), :] for k in range(TERMS)]
    work = dict(gram)
    for i in range(TERMS):
        work[i, i] = work[i, i] + 1.0
    right = [cross[k] if base is None else cross[k] - base[k] for k in range(TERMS)]
    inverse, factor = [], {}
    for i in range(TERMS):
        inv = 1.0 / work[i, i]
        inverse.append(inv)
        for r in range(i + 1, TERMS):
            factor[r, i] = work[i, r] * inv
        for r in range(i + 1, TERMS):
            for c in range(r, TERMS):
                work[r, c] = work[r, c] - factor[r, i] * work[i, c]
            right[r] = right[r] - factor[r, i] * right[i]
    answer = [None] * TERMS
    for i in reversed(range(TERMS)):
        value = right[i] * inverse[i]
        for c in range(i + 1, TERMS):
            value = value - factor[c, i] * answer[c]
        answer[i] = value
    lost = None
    for i in range(TERMS):
        image = None
        for c in range(TERMS):
            part = gram[min(i, c), max(i, c)] * answer[c]
            image = part if image is None else image + part
        part = answer[i] * (2.0 * cross[i] - image)
        lost = part if lost is None else lost + part
    sub = lax.broadcasted_iota(jnp.int32, (8, 128), 0)
    lost = jnp.sum(jnp.where(sub < BANDS, lost, 0.0), axis=0, keepdims=True)
    spread = jnp.maximum(mom(EXTRA_S) - jnp.broadcast_to(lost, (8, 128)), 0.0) * (1.0 / BANDS)
    return answer, spread / (1.0 + mom(0))


def swap_halo(variance, own_ref, near_ref, sems):
    send, recv = sems
    s, j, x, z = place()
    own_ref[...] = variance
    copies = []
    for n, (a, b) in enumerate(NEIGHBOURS):
        back = NEIGHBOURS.index((-a, -b))
        copy = copy_to(
            own_ref, near_ref.at[back], send.at[n], recv.at[back], wrap(s + a, 16), wrap(j + b, SHARDS)
        )
        copy.start()
        copies.append(copy)
    return copies


def box_mean(variance, near_ref, copies):
    s, j, x, z = place()
    for copy in copies:
        copy.wait()
    lane = lax.broadcasted_iota(jnp.int32, (8, 128), 1)
    col, row = lane % 16, lane // 16

    def field(a, b):
        if (a, b) == (0, 0):
            return variance
        value = near_ref[NEIGHBOURS.index((a, b))]
        inside = jnp.int32(1)
        if a:
            inside = inside * ((s + a >= 0) & (s + a < 16)).astype(jnp.int32)
        if b:
            inside = inside * ((j + b >= 0) & (j + b < SHARDS)).astype(jnp.int32)
        return jnp.where(jnp.full((8, 128), inside) > 0, value, 0.0)

    across = []
    for a in (-1, 0, 1):
        middle = field(a, 0)
        left = pltpu.roll(field(a, -1), 128 - 16, 1)
        right = pltpu.roll(field(a, 1), 16, 1)
        total = middle
        for step in (1, 2):
            total = total + pltpu.roll(jnp.where(col < step, right, middle), 128 - step, 1)
            total = total + pltpu.roll(jnp.where(col >= 16 - step, left, middle), step, 1)
        across.append(total)
    up, middle, down = across
    total = middle
    for step in (1, 2):
        total = total + pltpu.roll(jnp.where(row < step, down, middle), 128 - 16 * step, 1)
        total = total + pltpu.roll(jnp.where(row >= 8 - step, up, middle), 16 * step, 1)

    def count(index, whole):
        return (jnp.minimum(index + 2, whole - 1) - jnp.maximum(index - 2, 0) + 1).astype(F32)

    return total / (count(s * 8 + row, 128) * count(j * 16 + col, COLS))


def whole(
    dates, days_ref, obs_hbm, valid_hbm, out_ref,
    obs_ref, valid_ref, turned_ref, day_ref, table_ref, mask_ref, w_ref, s_ref, r_ref, block_ref,
    in_sem, trade_send, trade_recv, sp_send, sp_recv, *rest,
):
    s, j, x, z = place()
    own = pl.ds(pl.multiple_of(x * WIDE, 128), WIDE)
    other = pl.ds(pl.multiple_of((1 - x) * WIDE, 128), WIDE)
    early, late = pl.ds(0, dates), pl.ds(dates, dates)
    valid_copies = [
        pltpu.make_async_copy(valid_hbm.at[:, :, cols], valid_ref.at[n], in_sem.at[BANDS + n])
        for n, cols in ((1, other), (0, own))
    ]
    obs_copies = [
        pltpu.make_async_copy(obs_hbm.at[b, :, :, own], obs_ref.at[b, early], in_sem.at[b]) for b in range(BANDS)
    ]
    for copy in valid_copies + obs_copies:
        copy.start()
    barrier, guests = greet()
    partner = (s, (1 - x) * ZS + z)

    def trade(n, src, dst):
        return copy_to(src, dst, trade_send.at[n], trade_recv.at[n], *partner)

    trades = [
        trade(b, obs_hbm.at[b, :, :, other], obs_ref.at[b, late]) for b in range(BANDS)
    ]
    day_trade = trade(BANDS, day_ref.at[early], day_ref.at[late])
    mask_trade = trade(BANDS + 1, turned_ref.at[0], turned_ref.at[1])
    rows = lax.broadcasted_iota(jnp.int32, (dates, 128), 0)
    day = jnp.zeros((dates, 128), F32)
    for d in range(dates):
        day = jnp.where(rows == d, days_ref[d].astype(F32), day)
    day_ref[0:dates, :] = day
    valid_copies[0].wait()

    @pl.loop(0, dates)
    def _(d):
        turned_ref[0, d] = valid_ref[1, d].astype(F32).astype(jnp.bfloat16)

    design_table(dates, 0, day_ref, table_ref)
    pl.semaphore_wait(barrier, guests)
    day_trade.start()
    mask_trade.start()
    for copy in trades:
        copy.start()
    valid_copies[1].wait()

    @pl.loop(0, dates)
    def _(d):
        mask_ref[d] = valid_ref[0, d].astype(F32)

    day_trade.wait_recv()
    design_table(dates, dates, day_ref, table_ref)
    mask_trade.wait_recv()

    @pl.loop(0, dates)
    def _(d):
        mask_ref[dates + d] = turned_ref[1, d].astype(F32)

    reductions, halos = [], []
    for n in range(2):
        part = rest[12 * n : 12 * n + 12]
        reductions.append(Reduction(part[:4], part[4], part[5], part[8:10], (SLOW_PLAN, FAST_PLAN)[n]))
        halos.append((part[6], part[7], part[10:12]))

    def ready(b):
        obs_copies[b].wait()
        trades[b].wait_recv()

    both = 2 * dates
    first, last = reductions
    form_moments(
        both, lambda b, d, q: obs_ref[b, d, :, tile(q)].astype(F32), mask_ref, table_ref, s_ref, first.mom,
        ready, first.advance,
    )
    first.run()
    answer, variance = solve(first.mine, None)
    own_ref, near_ref, halo_sems = halos[0]
    copies = swap_halo(variance, own_ref, near_ref, halo_sems)
    base_row = pl.multiple_of(z * BLOCK, 8)
    for k in range(TERMS):
        block_ref[pl.ds(base_row + k, 8, stride=8), :] = answer[k]
    spread = Spread(block_ref, (sp_send, sp_recv))
    spread.begin(0)
    spread.begin(1)
    spread.relay(0, 1)
    spread.relay(1, 1)
    smooth = box_mean(variance, near_ref, copies)
    block_ref[pl.ds(pl.multiple_of(base_row + 8 * BANDS, 8), 8), :] = smooth
    spread.begin(2)
    for n, step in ((0, 2), (1, 2), (0, 3), (1, 3), (2, 1), (0, 4), (1, 4)):
        spread.relay(n, step)
    form_residuals(
        both, obs_ref, mask_ref, table_ref, block_ref, r_ref, w_ref, lambda: spread.relay(2, 2)
    )
    form_moments(
        both, lambda b, d, q: r_ref[b, d, :, tile(q)], w_ref, table_ref, s_ref, last.mom,
        lambda b: None, last.advance,
    )
    last.run()
    base = [block_ref[pl.ds(base_row + k, 8, stride=8), :] for k in range(TERMS)]
    answer, variance = solve(last.mine, base)
    own_ref, near_ref, halo_sems = halos[1]
    copies = swap_halo(variance, own_ref, near_ref, halo_sems)
    masks = flip_masks()
    for k in range(TERMS):
        turned = flip(base[k] + answer[k], masks)
        for b in range(BANDS):
            out_ref[b * TERMS + k] = (turned if b == 0 else pltpu.roll(turned, 128 - 16 * b, 1))[:, :16]
    spread.drain()
    first.drain()
    last.drain()
    for copy in trades + [day_trade, mask_trade]:
        copy.wait_send()
    smooth = box_mean(variance, near_ref, copies)
    out_ref[BANDS * TERMS] = flip(jnp.sqrt(smooth + EPS), masks)[:, :16]


def reduction_scratch():
    ring, eight = pltpu.SemaphoreType.DMA((8, 4, len(PIECES))), pltpu.SemaphoreType.DMA((8,))
    return [
        *[pltpu.VMEM((ZS * count, 128), F32) for _, count in PIECES],
        pltpu.VMEM((8, 4, DEEP, 128), F32),
        pltpu.VMEM((DEEP, 128), F32),
        pltpu.VMEM((8, 128), F32),
        pltpu.VMEM((8, 8, 128), F32),
        ring, ring, eight, eight,
    ]


def on_device(obs, valid, days):
    dates = obs.shape[1]
    spread = pltpu.SemaphoreType.DMA((8, 4, len(PARTS)))
    trade = pltpu.SemaphoreType.DMA((BANDS + 2,))
    out = pl.pallas_call(
        functools.partial(whole, dates),
        out_shape=jax.ShapeDtypeStruct((BANDS * TERMS + 1, ROWS, 16), F32),
        in_specs=[
            pl.BlockSpec(memory_space=pltpu.SMEM),
            pl.BlockSpec(memory_space=pl.ANY),
            pl.BlockSpec(memory_space=pl.ANY),
        ],
        out_specs=pl.BlockSpec(memory_space=pltpu.VMEM),
        scratch_shapes=[
            pltpu.VMEM((BANDS, 2 * dates, ROWS, WIDE), jnp.bfloat16),
            pltpu.VMEM((2, dates, ROWS, WIDE), jnp.int32),
            pltpu.VMEM((2, dates, ROWS, WIDE), jnp.bfloat16),
            pltpu.VMEM((2 * dates, 128), F32),
            pltpu.VMEM((2 * dates * FIELDS, 128), F32),
            pltpu.VMEM((2 * dates, ROWS, WIDE), F32),
            pltpu.VMEM((2 * dates, ROWS, WIDE), F32),
            pltpu.VMEM((ROWS, WIDE), F32),
            pltpu.VMEM((BANDS, 2 * dates, ROWS, WIDE), F32),
            pltpu.VMEM((ZS * BLOCK, 128), F32),
            pltpu.SemaphoreType.DMA((BANDS + 2,)),
            trade, trade, spread, spread,
            *reduction_scratch(),
            *reduction_scratch(),
        ],
        compiler_params=pltpu.CompilerParams(collective_id=0, has_side_effects=True, vmem_limit_bytes=56 << 20),
    )(days, obs, valid)
    return out[: BANDS * TERMS].reshape(BANDS, TERMS, ROWS, 16), out[BANDS * TERMS]


def solution(mesh):
    in_specs = (P(None, "date", "space", None), P("date", "space", None), P("date"))
    out_specs = (P(None, None, "space", "date"), P("space", "date"))
    return jax.shard_map(on_device, mesh=mesh, in_specs=in_specs, out_specs=out_specs, check_vma=False)
```

```python
import functools
import math

import jax
import jax.numpy as jnp
from jax import lax
from jax.experimental import pallas as pl
from jax.experimental.pallas import tpu as pltpu
from jax.sharding import PartitionSpec as P

F32 = jnp.float32
MESH = pl.DeviceIdType.MESH
TUKEY = 4.685
EPS = 1e-06
BANDS = 7
TERMS = 8
ROWS = 8
COLS = 512
WIDE = 256
TILES = 2
SHARDS = 32
DEEP = 80
BLOCK = 64
FIELDS = 24
ZS = 16
UNROLL = 8

C0, S0, TC0, TS0, EXTRA_S = 2, 8, 14, 17, 21
NEIGHBOURS = [(a, b) for a in (-1, 0, 1) for b in (-1, 0, 1) if (a, b) != (0, 0)]
PIECES = ((64, 16), (0, 16), (16, 24), (40, 24))
BY_TWO = ((1, 8, 2), (1, 7, 2), (-1, 7, 2), (-1, 6, 2))
BY_FOUR = tuple((1, n, 4) for n in (8, 7, 6, 5)) + tuple((-1, n, 4) for n in (7, 6, 5, 4))
CHAINS = (BY_TWO, BY_TWO, BY_TWO, BY_FOUR)
SLOW_PLAN = (
    ((0, 0),),
    ((1, 0), (0, 1)),
    ((2, 0), (1, 1), (0, 2)),
    ((3, 0),),
    ((0, 3), (1, 2), (2, 1), (0, 4), (1, 3), (2, 2), (3, 1), (1, 4), (2, 3), (3, 2), (2, 4)),
)
FAST_PLAN = (
    ((0, 0),),
    ((1, 0),),
    ((2, 0),),
    ((3, 0),),
    ((0, 1), (1, 1), (2, 1), (0, 2), (1, 2), (3, 1), (2, 2), (0, 3), (1, 3), (2, 3), (0, 4), (1, 4), (3, 2), (2, 4)),
)
OUT_BY_TWO = ((1, 2, 4, 2), (1, 1, 4, 2), (-1, 1, 4, 2), (-1, 2, 3, 2))
OUT_BY_FOUR = tuple((1, n, 2, 4) for n in (4, 3, 2, 1)) + tuple((-1, n, 2 if n < 4 else 1, 4) for n in (4, 3, 2, 1))
SPREADS = (OUT_BY_TWO, OUT_BY_TWO, OUT_BY_FOUR)
PARTS = ((0, 32), (32, 24), (56, 8))


def extra_row(e):
    return 64 + e if e < 16 else 40 + e


def gram_terms(i, j):
    if i > j:
        i, j = j, i
    if i == 0:
        if j < 2:
            return [(1.0, j)]
        n = j // 2
        return [(1.0, (C0 if j % 2 == 0 else S0) + n)]
    if i == 1:
        if j == 1:
            return [(1.0, 2)]
        n = j // 2
        return [(1.0, (TC0 if j % 2 == 0 else TS0) + n)]
    a, b = i // 2, j // 2

    def cosine(n):
        return 0 if n == 0 else C0 + n

    if i % 2 == 0 and j % 2 == 0:
        return [(0.5, cosine(abs(a - b))), (0.5, cosine(a + b))]
    if i % 2 == 1 and j % 2 == 1:
        return [(0.5, cosine(abs(a - b))), (-0.5, cosine(a + b))]
    s, c = (a, b) if i % 2 == 1 else (b, a)
    terms = [(0.5, S0 + s + c)]
    if s != c:
        terms.append((0.5 if s > c else -0.5, S0 + abs(s - c)))
    return terms


def turn(angle):
    turns = jnp.floor(angle * (0.5 / math.pi) + 0.5)
    half = 0.5 * ((angle - turns * 6.28125) - turns * (2.0 * math.pi - 6.28125))
    square = half * half
    s = jnp.full_like(half, 1.0 / math.factorial(13))
    for n in (11, 9, 7, 5, 3, 1):
        s = s * square + (1.0 if n % 4 == 1 else -1.0) / math.factorial(n)
    s = s * half
    c = jnp.full_like(half, 1.0 / math.factorial(12))
    for n in (10, 8, 6, 4, 2, 0):
        c = c * square + (1.0 if n % 4 == 0 else -1.0) / math.factorial(n)
    return 1.0 - 2.0 * s * s, 2.0 * s * c


def design_table(dates, first_date, day_ref, table_ref):
    day = day_ref[first_date : first_date + dates, :]
    t = (day - 1825.0) / 1825.0
    c1, s1 = turn(day * (2.0 * math.pi / 365.25))
    c, s = [None, c1, 1 - 2 * s1 * s1], [None, s1, 2 * s1 * c1]
    c.append(c1 * c[2] - s1 * s[2])
    s.append(s1 * c[2] + c1 * s[2])
    c += [1 - 2 * s[2] * s[2], c[2] * c[3] - s[2] * s[3], 1 - 2 * s[3] * s[3]]
    s += [2 * s[2] * c[2], s[2] * c[3] + c[2] * s[3], 2 * s[3] * c[3]]
    fields = [jnp.ones_like(t), t, t * t] + c[1:] + s[1:]
    fields += [t * c[h] for h in range(1, 4)] + [t * s[h] for h in range(1, 4)]
    for f, value in enumerate(fields):
        for first in range(0, dates, 8):
            start = (first_date + first) * FIELDS + f
            table_ref[pl.ds(start, 8, stride=FIELDS), :] = value[first : first + 8]


COLUMN = [0, 1, C0 + 1, S0 + 1, C0 + 2, S0 + 2, C0 + 3, S0 + 3]


def flip_masks():
    sub = lax.broadcasted_iota(jnp.int32, (8, 128), 0)
    group = lax.broadcasted_iota(jnp.int32, (8, 128), 1) // 16
    masks = []
    for bit in (4, 2, 1):
        s, g = (sub & bit) != 0, (group & bit) != 0
        masks.append((jnp.logical_and(s, jnp.logical_not(g)), jnp.logical_and(jnp.logical_not(s), g)))
    return masks


def flip(v, masks):
    for bit, (low, high) in zip((4, 2, 1), masks):
        up = pltpu.roll(pltpu.roll(v, bit, 0), 128 - 16 * bit, 1)
        if bit == 4:
            v = jnp.where(jnp.logical_or(low, high), up, v)
        else:
            down = pltpu.roll(pltpu.roll(v, 8 - bit, 0), 16 * bit, 1)
            v = jnp.where(low, up, jnp.where(high, down, v))
    return v


def tile(q):
    return slice(128 * q, 128 * q + 128)


def splat(table_ref, d, field):
    return table_ref[pl.ds(d * FIELDS + field, 8, stride=0), :]


def by_date(dates, one, carry):
    def body(n, carry):
        for u in range(UNROLL):
            carry = one(n * UNROLL + u, carry)
        return carry

    return lax.fori_loop(0, dates // UNROLL, body, carry)


def form_moments(dates, load, w_ref, table_ref, s_ref, out_refs, ready, done):
    masks = flip_masks()
    zero = jnp.zeros((8, 128), F32)

    def put(row, q, v):
        for (first, count), out_ref in zip(PIECES, out_refs):
            if first <= row < first + count:
                out_ref[pl.ds(q * 8 * count + row - first, 8, stride=count), :] = v

    for first in range(0, EXTRA_S, 11):
        fields = list(range(first, min(first + 11, EXTRA_S)))

        def one(d, acc):
            acc = list(acc)
            w = [w_ref[d, :, tile(q)] for q in range(TILES)]
            for n, e in enumerate(fields):
                x = splat(table_ref, d, e) if e else None
                for q in range(TILES):
                    acc[n * TILES + q] = acc[n * TILES + q] + (x * w[q] if e else w[q])
            return tuple(acc)

        acc = by_date(dates, one, (zero,) * (len(fields) * TILES))
        for n, e in enumerate(fields):
            for q in range(TILES):
                put(extra_row(e), q, flip(acc[n * TILES + q], masks))
    done(0)
    for b in range(BANDS):
        ready(b)

        def one(d, carry):
            acc, square = list(carry[0]), list(carry[1])
            wy = []
            for q in range(TILES):
                y = load(b, d, q)
                v = w_ref[d, :, tile(q)] * y
                square[q] = square[q] + v * y
                wy.append(v)
            for k in range(TERMS):
                x = splat(table_ref, d, COLUMN[k]) if k else None
                for q in range(TILES):
                    acc[k * TILES + q] = acc[k * TILES + q] + (x * wy[q] if k else wy[q])
            return tuple(acc), tuple(square)

        acc, square = by_date(dates, one, ((zero,) * (TERMS * TILES), (zero,) * TILES))
        for k in range(TERMS):
            for q in range(TILES):
                put(8 * b + k, q, flip(acc[k * TILES + q], masks))
        for q in range(TILES):
            total = square[q] if b == 0 else s_ref[:, tile(q)] + square[q]
            if b < BANDS - 1:
                s_ref[:, tile(q)] = total
            else:
                put(extra_row(EXTRA_S), q, flip(total, masks))
                for row in range(extra_row(EXTRA_S) + 1, 64):
                    put(row, q, zero)
        for n, (first, count) in enumerate(PIECES):
            if n and 8 * b + 8 == min(first + count, 8 * BANDS):
                done(n)


def form_residuals(dates, obs_ref, mask_ref, table_ref, block_ref, r_ref, w_ref, smooth_ready):
    masks = flip_masks()

    def get(row, q):
        return flip(block_ref[pl.ds(q * 8 * BLOCK + row, 8, stride=BLOCK), :], masks)

    for b in range(BANDS):
        beta = [[get(8 * b + k, q) for q in range(TILES)] for k in range(TERMS)]

        def one(d, carry):
            x = [splat(table_ref, d, COLUMN[k]) if k else None for k in range(TERMS)]
            for q in range(TILES):
                fit = beta[0][q]
                for k in range(1, TERMS):
                    fit = fit + x[k] * beta[k][q]
                r = obs_ref[b, d, :, tile(q)].astype(F32) - fit
                r_ref[b, d, :, tile(q)] = r
                if b == 0:
                    w_ref[d, :, tile(q)] = r * r
                else:
                    w_ref[d, :, tile(q)] = w_ref[d, :, tile(q)] + r * r
            return carry

        by_date(dates, one, 0)
    smooth_ready()
    scale = [1.0 / (float(BANDS) * (TUKEY * TUKEY) * (get(8 * BANDS, q) + EPS)) for q in range(TILES)]

    def weigh(d, carry):
        for q in range(TILES):
            left = 1.0 - jnp.minimum(w_ref[d, :, tile(q)] * scale[q], 1.0)
            w_ref[d, :, tile(q)] = mask_ref[d, :, tile(q)] * left * left
        return carry

    by_date(dates, weigh, 0)


def copy_to(src, dst, send, recv, space, date):
    return pltpu.make_async_remote_copy(
        src_ref=src, dst_ref=dst, send_sem=send, recv_sem=recv, device_id=(space, date), device_id_type=MESH
    )


def place():
    s, j = lax.axis_index("space"), lax.axis_index("date")
    return s, j, j // ZS, lax.rem(j, ZS)


def wrap(value, count):
    return lax.rem(value + count, count)


def greet():
    s, j, x, z = place()
    sem = pltpu.get_barrier_semaphore()
    targets = [(s, x * ZS + wrap(z + h, ZS)) for h in (1, -1, 2, -2, 3, -3, 4, -4)] + [(s, (1 - x) * ZS + z)]
    targets += [(wrap(s + a, 16), wrap(j + b, SHARDS)) for a, b in NEIGHBOURS]
    for target in targets:
        pl.semaphore_signal(sem, inc=1, device_id=target, device_id_type=MESH)
    return sem, len(targets)


class Reduction:
    def __init__(self, mom_refs, slot_ref, mine_ref, sems, plan):
        self.mom, self.slot, self.mine, self.plan = mom_refs, slot_ref, mine_ref, plan
        self.send, self.recv = sems
        self.s, self.j, self.x, self.z = place()

    def length(self, n, chain):
        _, first, stride = CHAINS[n][chain]
        return (first + stride - 1) // stride

    def rows(self, n, chain, step):
        way, first, stride = CHAINS[n][chain]
        count = PIECES[n][1]
        return pl.ds(pl.multiple_of(wrap(self.z + way * (first - stride * step), ZS) * count, 8), count)

    def place_of(self, n, chain, step):
        return self.slot.at[chain, step, pl.ds(*PIECES[n])]

    def hop(self, n, chain, step):
        way, first, stride = CHAINS[n][chain]
        reach = min(stride, first - stride * step)
        source = self.mom[n].at[self.rows(n, chain, 0)] if step == 0 else self.place_of(n, chain, step - 1)
        return copy_to(
            source, self.place_of(n, chain, step), self.send.at[chain, step, n], self.recv.at[chain, step, n],
            self.s, self.x * ZS + wrap(self.z + way * reach, ZS),
        )

    def step(self, n, step):
        for chain in range(len(CHAINS[n])):
            if step >= self.length(n, chain):
                continue
            if step:
                self.hop(n, chain, step - 1).wait_recv()
                here = self.place_of(n, chain, step - 1)
                here[...] = here[...] + self.mom[n][self.rows(n, chain, step), :]
            self.hop(n, chain, step).start()

    def finish(self, n):
        first, count = PIECES[n]
        total = self.mom[n][pl.ds(pl.multiple_of(self.z * count, 8), count), :]
        for chain in range(len(CHAINS[n])):
            last = self.length(n, chain) - 1
            self.hop(n, chain, last).wait_recv()
            total = total + self.slot[chain, last, pl.ds(first, count), :]
        self.mine[pl.ds(first, count), :] = total

    def advance(self, stage):
        for n, step in self.plan[stage]:
            if step == max(self.length(n, chain) for chain in range(len(CHAINS[n]))):
                self.finish(n)
            else:
                self.step(n, step)

    def run(self):
        self.advance(len(PIECES))

    def drain(self):
        for n in range(len(PIECES)):
            for chain in range(len(CHAINS[n])):
                for step in range(self.length(n, chain)):
                    self.hop(n, chain, step).wait_send()


class Spread:
    def __init__(self, block_ref, sems):
        self.block = block_ref
        self.send, self.recv = sems
        self.s, self.j, self.x, self.z = place()

    def piece(self, owner, n):
        first, count = PARTS[n]
        return self.block.at[pl.ds(pl.multiple_of(wrap(owner + ZS, ZS) * BLOCK + first, 8), count)]

    def offset(self, n, chain, step):
        way, first, _, stride = SPREADS[n][chain]
        return 0 if step == 0 else way * (first + stride * (step - 1))

    def hop(self, n, chain, step):
        way, first, _, stride = SPREADS[n][chain]
        reach = first if step == 0 else stride
        piece = self.piece(self.z - self.offset(n, chain, step), n)
        return copy_to(
            piece, piece, self.send.at[chain, step, n], self.recv.at[chain, step, n],
            self.s, self.x * ZS + wrap(self.z + way * reach, ZS),
        )

    def arrival(self, n, chain, step):
        piece = self.piece(self.z - self.offset(n, chain, step + 1), n)
        return copy_to(
            piece, piece, self.send.at[chain, step, n], self.recv.at[chain, step, n], self.s, self.j
        )

    def begin(self, n):
        for chain in range(len(SPREADS[n])):
            self.hop(n, chain, 0).start()

    def relay(self, n, step):
        for chain in range(len(SPREADS[n])):
            if step <= SPREADS[n][chain][2]:
                self.arrival(n, chain, step - 1).wait_recv()
                if step < SPREADS[n][chain][2]:
                    self.hop(n, chain, step).start()

    def drain(self):
        for n in range(len(PARTS)):
            for chain in range(len(SPREADS[n])):
                for step in range(SPREADS[n][chain][2]):
                    self.hop(n, chain, step).wait_send()


def solve(mine_ref, base):
    moment = {}

    def mom(e):
        if e not in moment:
            moment[e] = jnp.broadcast_to(mine_ref[extra_row(e) : extra_row(e) + 1, :], (8, 128))
        return moment[e]

    gram = {}
    for i in range(TERMS):
        for j in range(i, TERMS):
            value = None
            for factor, e in gram_terms(i, j):
                part = mom(e) if factor == 1.0 else factor * mom(e)
                value = part if value is None else value + part
            gram[i, j] = value
    cross = [mine_ref[pl.ds(k, 8, stride=8), :] for k in range(TERMS)]
    work = dict(gram)
    for i in range(TERMS):
        work[i, i] = work[i, i] + 1.0
    right = [cross[k] if base is None else cross[k] - base[k] for k in range(TERMS)]
    inverse, factor = [], {}
    for i in range(TERMS):
        inv = 1.0 / work[i, i]
        inverse.append(inv)
        for r in range(i + 1, TERMS):
            factor[r, i] = work[i, r] * inv
        for r in range(i + 1, TERMS):
            for c in range(r, TERMS):
                work[r, c] = work[r, c] - factor[r, i] * work[i, c]
            right[r] = right[r] - factor[r, i] * right[i]
    answer = [None] * TERMS
    for i in reversed(range(TERMS)):
        value = right[i] * inverse[i]
        for c in range(i + 1, TERMS):
            value = value - factor[c, i] * answer[c]
        answer[i] = value
    lost = None
    for i in range(TERMS):
        image = None
        for c in range(TERMS):
            part = gram[min(i, c), max(i, c)] * answer[c]
            image = part if image is None else image + part
        part = answer[i] * (2.0 * cross[i] - image)
        lost = part if lost is None else lost + part
    sub = lax.broadcasted_iota(jnp.int32, (8, 128), 0)
    lost = jnp.sum(jnp.where(sub < BANDS, lost, 0.0), axis=0, keepdims=True)
    spread = jnp.maximum(mom(EXTRA_S) - jnp.broadcast_to(lost, (8, 128)), 0.0) * (1.0 / BANDS)
    return answer, spread / (1.0 + mom(0))


def swap_halo(variance, own_ref, near_ref, sems):
    send, recv = sems
    s, j, x, z = place()
    own_ref[...] = variance
    copies = []
    for n, (a, b) in enumerate(NEIGHBOURS):
        back = NEIGHBOURS.index((-a, -b))
        copy = copy_to(
            own_ref, near_ref.at[back], send.at[n], recv.at[back], wrap(s + a, 16), wrap(j + b, SHARDS)
        )
        copy.start()
        copies.append(copy)
    return copies


def box_mean(variance, near_ref, copies):
    s, j, x, z = place()
    for copy in copies:
        copy.wait()
    lane = lax.broadcasted_iota(jnp.int32, (8, 128), 1)
    col, row = lane % 16, lane // 16

    def field(a, b):
        if (a, b) == (0, 0):
            return variance
        value = near_ref[NEIGHBOURS.index((a, b))]
        inside = jnp.int32(1)
        if a:
            inside = inside * ((s + a >= 0) & (s + a < 16)).astype(jnp.int32)
        if b:
            inside = inside * ((j + b >= 0) & (j + b < SHARDS)).astype(jnp.int32)
        return jnp.where(jnp.full((8, 128), inside) > 0, value, 0.0)

    across = []
    for a in (-1, 0, 1):
        middle = field(a, 0)
        left = pltpu.roll(field(a, -1), 128 - 16, 1)
        right = pltpu.roll(field(a, 1), 16, 1)
        total = middle
        for step in (1, 2):
            total = total + pltpu.roll(jnp.where(col < step, right, middle), 128 - step, 1)
            total = total + pltpu.roll(jnp.where(col >= 16 - step, left, middle), step, 1)
        across.append(total)
    up, middle, down = across
    total = middle
    for step in (1, 2):
        total = total + pltpu.roll(jnp.where(row < step, down, middle), 128 - 16 * step, 1)
        total = total + pltpu.roll(jnp.where(row >= 8 - step, up, middle), 16 * step, 1)

    def count(index, whole):
        return (jnp.minimum(index + 2, whole - 1) - jnp.maximum(index - 2, 0) + 1).astype(F32)

    return total / (count(s * 8 + row, 128) * count(j * 16 + col, COLS))


def whole(
    dates, days_ref, obs_hbm, valid_hbm, out_ref,
    obs_ref, valid_ref, turned_ref, day_ref, table_ref, mask_ref, w_ref, s_ref, r_ref, block_ref,
    in_sem, trade_send, trade_recv, sp_send, sp_recv, *rest,
):
    s, j, x, z = place()
    own = pl.ds(pl.multiple_of(x * WIDE, 128), WIDE)
    other = pl.ds(pl.multiple_of((1 - x) * WIDE, 128), WIDE)
    early, late = pl.ds(0, dates), pl.ds(dates, dates)
    valid_copies = [
        pltpu.make_async_copy(valid_hbm.at[:, :, cols], valid_ref.at[n], in_sem.at[BANDS + n])
        for n, cols in ((1, other), (0, own))
    ]
    obs_copies = [
        pltpu.make_async_copy(obs_hbm.at[b, :, :, own], obs_ref.at[b, early], in_sem.at[b]) for b in range(BANDS)
    ]
    for copy in valid_copies + obs_copies:
        copy.start()
    barrier, guests = greet()
    partner = (s, (1 - x) * ZS + z)

    def trade(n, src, dst):
        return copy_to(src, dst, trade_send.at[n], trade_recv.at[n], *partner)

    trades = [
        trade(b, obs_hbm.at[b, :, :, other], obs_ref.at[b, late]) for b in range(BANDS)
    ]
    day_trade = trade(BANDS, day_ref.at[early], day_ref.at[late])
    mask_trade = trade(BANDS + 1, turned_ref.at[0], turned_ref.at[1])
    rows = lax.broadcasted_iota(jnp.int32, (dates, 128), 0)
    day = jnp.zeros((dates, 128), F32)
    for d in range(dates):
        day = jnp.where(rows == d, days_ref[d].astype(F32), day)
    day_ref[0:dates, :] = day
    valid_copies[0].wait()

    @pl.loop(0, dates)
    def _(d):
        turned_ref[0, d] = valid_ref[1, d].astype(F32).astype(jnp.bfloat16)

    design_table(dates, 0, day_ref, table_ref)
    pl.semaphore_wait(barrier, guests)
    day_trade.start()
    mask_trade.start()
    for copy in trades:
        copy.start()
    valid_copies[1].wait()

    @pl.loop(0, dates)
    def _(d):
        mask_ref[d] = valid_ref[0, d].astype(F32)

    day_trade.wait_recv()
    design_table(dates, dates, day_ref, table_ref)
    mask_trade.wait_recv()

    @pl.loop(0, dates)
    def _(d):
        mask_ref[dates + d] = turned_ref[1, d].astype(F32)

    reductions, halos = [], []
    for n in range(2):
        part = rest[12 * n : 12 * n + 12]
        reductions.append(Reduction(part[:4], part[4], part[5], part[8:10], (SLOW_PLAN, FAST_PLAN)[n]))
        halos.append((part[6], part[7], part[10:12]))

    def ready(b):
        obs_copies[b].wait()
        trades[b].wait_recv()

    both = 2 * dates
    first, last = reductions
    form_moments(
        both, lambda b, d, q: obs_ref[b, d, :, tile(q)].astype(F32), mask_ref, table_ref, s_ref, first.mom,
        ready, first.advance,
    )
    first.run()
    answer, variance = solve(first.mine, None)
    own_ref, near_ref, halo_sems = halos[0]
    copies = swap_halo(variance, own_ref, near_ref, halo_sems)
    base_row = pl.multiple_of(z * BLOCK, 8)
    for k in range(TERMS):
        block_ref[pl.ds(base_row + k, 8, stride=8), :] = answer[k]
    spread = Spread(block_ref, (sp_send, sp_recv))
    spread.begin(0)
    spread.begin(1)
    spread.relay(0, 1)
    spread.relay(1, 1)
    smooth = box_mean(variance, near_ref, copies)
    block_ref[pl.ds(pl.multiple_of(base_row + 8 * BANDS, 8), 8), :] = smooth
    spread.begin(2)
    for n, step in ((0, 2), (1, 2), (0, 3), (1, 3), (2, 1), (0, 4), (1, 4)):
        spread.relay(n, step)
    form_residuals(
        both, obs_ref, mask_ref, table_ref, block_ref, r_ref, w_ref, lambda: spread.relay(2, 2)
    )
    form_moments(
        both, lambda b, d, q: r_ref[b, d, :, tile(q)], w_ref, table_ref, s_ref, last.mom,
        lambda b: None, last.advance,
    )
    last.run()
    base = [block_ref[pl.ds(base_row + k, 8, stride=8), :] for k in range(TERMS)]
    answer, variance = solve(last.mine, base)
    own_ref, near_ref, halo_sems = halos[1]
    copies = swap_halo(variance, own_ref, near_ref, halo_sems)
    masks = flip_masks()
    for k in range(TERMS):
        turned = flip(base[k] + answer[k], masks)
        for b in range(BANDS):
            out_ref[b * TERMS + k] = (turned if b == 0 else pltpu.roll(turned, 128 - 16 * b, 1))[:, :16]
    spread.drain()
    first.drain()
    last.drain()
    for copy in trades + [day_trade, mask_trade]:
        copy.wait_send()
    smooth = box_mean(variance, near_ref, copies)
    out_ref[BANDS * TERMS] = flip(jnp.sqrt(smooth + EPS), masks)[:, :16]


def part_outputs(out_ref, coef_ref, noise_ref):
    for b in range(BANDS):
        coef_ref[b] = out_ref[b * TERMS : (b + 1) * TERMS]
    noise_ref[...] = out_ref[BANDS * TERMS]


def reduction_scratch():
    ring, eight = pltpu.SemaphoreType.DMA((8, 4, len(PIECES))), pltpu.SemaphoreType.DMA((8,))
    return [
        *[pltpu.VMEM((ZS * count, 128), F32) for _, count in PIECES],
        pltpu.VMEM((8, 4, DEEP, 128), F32),
        pltpu.VMEM((DEEP, 128), F32),
        pltpu.VMEM((8, 128), F32),
        pltpu.VMEM((8, 8, 128), F32),
        ring, ring, eight, eight,
    ]


def on_device(obs, valid, days):
    dates = obs.shape[1]
    spread = pltpu.SemaphoreType.DMA((8, 4, len(PARTS)))
    trade = pltpu.SemaphoreType.DMA((BANDS + 2,))
    out = pl.pallas_call(
        functools.partial(whole, dates),
        out_shape=jax.ShapeDtypeStruct((BANDS * TERMS + 1, ROWS, 16), F32),
        in_specs=[
            pl.BlockSpec(memory_space=pltpu.SMEM),
            pl.BlockSpec(memory_space=pl.ANY),
            pl.BlockSpec(memory_space=pl.ANY),
        ],
        out_specs=pl.BlockSpec(memory_space=pltpu.VMEM),
        scratch_shapes=[
            pltpu.VMEM((BANDS, 2 * dates, ROWS, WIDE), jnp.bfloat16),
            pltpu.VMEM((2, dates, ROWS, WIDE), jnp.int32),
            pltpu.VMEM((2, dates, ROWS, WIDE), jnp.bfloat16),
            pltpu.VMEM((2 * dates, 128), F32),
            pltpu.VMEM((2 * dates * FIELDS, 128), F32),
            pltpu.VMEM((2 * dates, ROWS, WIDE), F32),
            pltpu.VMEM((2 * dates, ROWS, WIDE), F32),
            pltpu.VMEM((ROWS, WIDE), F32),
            pltpu.VMEM((BANDS, 2 * dates, ROWS, WIDE), F32),
            pltpu.VMEM((ZS * BLOCK, 128), F32),
            pltpu.SemaphoreType.DMA((BANDS + 2,)),
            trade, trade, spread, spread,
            *reduction_scratch(),
            *reduction_scratch(),
        ],
        compiler_params=pltpu.CompilerParams(collective_id=0, has_side_effects=True, vmem_limit_bytes=56 << 20),
    )(days, obs, valid)
    return pl.pallas_call(
        part_outputs,
        out_shape=(
            jax.ShapeDtypeStruct((BANDS, TERMS, ROWS, 16), F32),
            jax.ShapeDtypeStruct((ROWS, 16), F32),
        ),
        in_specs=[pl.BlockSpec(memory_space=pltpu.VMEM)],
        out_specs=(pl.BlockSpec(memory_space=pltpu.VMEM), pl.BlockSpec(memory_space=pltpu.VMEM)),
    )(out)


def solution(mesh):
    in_specs = (P(None, "date", "space", None), P("date", "space", None), P("date"))
    out_specs = (P(None, None, "space", "date"), P("space", "date"))
    return jax.shard_map(on_device, mesh=mesh, in_specs=in_specs, out_specs=out_specs, check_vma=False)
```

```python
import functools
import math

import jax
import jax.numpy as jnp
from jax import lax
from jax.experimental import pallas as pl
from jax.experimental.pallas import tpu as pltpu
from jax.sharding import PartitionSpec as P

F32 = jnp.float32
MESH = pl.DeviceIdType.MESH
TUKEY = 4.685
EPS = 1e-06
BANDS = 7
TERMS = 8
ROWS = 8
COLS = 512
WIDE = 256
TILES = 2
SHARDS = 32
DEEP = 80
BLOCK = 64
FIELDS = 24
ZS = 16
UNROLL = 16

C0, S0, TC0, TS0, EXTRA_S = 2, 8, 14, 17, 21
NEIGHBOURS = [(a, b) for a in (-1, 0, 1) for b in (-1, 0, 1) if (a, b) != (0, 0)]
PIECES = ((64, 16), (0, 16), (16, 24), (40, 24))
BY_TWO = ((1, 8, 2), (1, 7, 2), (-1, 7, 2), (-1, 6, 2))
BY_FOUR = tuple((1, n, 4) for n in (8, 7, 6, 5)) + tuple((-1, n, 4) for n in (7, 6, 5, 4))
CHAINS = (BY_TWO, BY_TWO, BY_TWO, BY_FOUR)
SLOW_PLAN = (
    ((0, 0),),
    ((1, 0), (0, 1)),
    ((2, 0), (1, 1), (0, 2)),
    ((3, 0),),
    ((0, 3), (1, 2), (2, 1), (0, 4), (1, 3), (2, 2), (3, 1), (1, 4), (2, 3), (3, 2), (2, 4)),
)
FAST_PLAN = (
    ((0, 0),),
    ((1, 0),),
    ((2, 0),),
    ((3, 0),),
    ((0, 1), (1, 1), (2, 1), (0, 2), (1, 2), (3, 1), (2, 2), (0, 3), (1, 3), (2, 3), (0, 4), (1, 4), (3, 2), (2, 4)),
)
OUT_BY_TWO = ((1, 2, 4, 2), (1, 1, 4, 2), (-1, 1, 4, 2), (-1, 2, 3, 2))
OUT_BY_FOUR = tuple((1, n, 2, 4) for n in (4, 3, 2, 1)) + tuple((-1, n, 2 if n < 4 else 1, 4) for n in (4, 3, 2, 1))
SPREADS = (OUT_BY_TWO, OUT_BY_TWO, OUT_BY_FOUR)
PARTS = ((0, 32), (32, 24), (56, 8))


def extra_row(e):
    return 64 + e if e < 16 else 40 + e


def gram_terms(i, j):
    if i > j:
        i, j = j, i
    if i == 0:
        if j < 2:
            return [(1.0, j)]
        n = j // 2
        return [(1.0, (C0 if j % 2 == 0 else S0) + n)]
    if i == 1:
        if j == 1:
            return [(1.0, 2)]
        n = j // 2
        return [(1.0, (TC0 if j % 2 == 0 else TS0) + n)]
    a, b = i // 2, j // 2

    def cosine(n):
        return 0 if n == 0 else C0 + n

    if i % 2 == 0 and j % 2 == 0:
        return [(0.5, cosine(abs(a - b))), (0.5, cosine(a + b))]
    if i % 2 == 1 and j % 2 == 1:
        return [(0.5, cosine(abs(a - b))), (-0.5, cosine(a + b))]
    s, c = (a, b) if i % 2 == 1 else (b, a)
    terms = [(0.5, S0 + s + c)]
    if s != c:
        terms.append((0.5 if s > c else -0.5, S0 + abs(s - c)))
    return terms


def turn(angle):
    turns = jnp.floor(angle * (0.5 / math.pi) + 0.5)
    half = 0.5 * ((angle - turns * 6.28125) - turns * (2.0 * math.pi - 6.28125))
    square = half * half
    s = jnp.full_like(half, 1.0 / math.factorial(13))
    for n in (11, 9, 7, 5, 3, 1):
        s = s * square + (1.0 if n % 4 == 1 else -1.0) / math.factorial(n)
    s = s * half
    c = jnp.full_like(half, 1.0 / math.factorial(12))
    for n in (10, 8, 6, 4, 2, 0):
        c = c * square + (1.0 if n % 4 == 0 else -1.0) / math.factorial(n)
    return 1.0 - 2.0 * s * s, 2.0 * s * c


def design_table(dates, first_date, day_ref, table_ref):
    day = day_ref[first_date : first_date + dates, :]
    t = (day - 1825.0) / 1825.0
    c1, s1 = turn(day * (2.0 * math.pi / 365.25))
    c, s = [None, c1, 1 - 2 * s1 * s1], [None, s1, 2 * s1 * c1]
    c.append(c1 * c[2] - s1 * s[2])
    s.append(s1 * c[2] + c1 * s[2])
    c += [1 - 2 * s[2] * s[2], c[2] * c[3] - s[2] * s[3], 1 - 2 * s[3] * s[3]]
    s += [2 * s[2] * c[2], s[2] * c[3] + c[2] * s[3], 2 * s[3] * c[3]]
    fields = [jnp.ones_like(t), t, t * t] + c[1:] + s[1:]
    fields += [t * c[h] for h in range(1, 4)] + [t * s[h] for h in range(1, 4)]
    for f, value in enumerate(fields):
        for first in range(0, dates, 8):
            start = (first_date + first) * FIELDS + f
            table_ref[pl.ds(start, 8, stride=FIELDS), :] = value[first : first + 8]


COLUMN = [0, 1, C0 + 1, S0 + 1, C0 + 2, S0 + 2, C0 + 3, S0 + 3]


def flip_masks():
    sub = lax.broadcasted_iota(jnp.int32, (8, 128), 0)
    group = lax.broadcasted_iota(jnp.int32, (8, 128), 1) // 16
    masks = []
    for bit in (4, 2, 1):
        s, g = (sub & bit) != 0, (group & bit) != 0
        masks.append((jnp.logical_and(s, jnp.logical_not(g)), jnp.logical_and(jnp.logical_not(s), g)))
    return masks


def flip(v, masks):
    for bit, (low, high) in zip((4, 2, 1), masks):
        up = pltpu.roll(pltpu.roll(v, bit, 0), 128 - 16 * bit, 1)
        if bit == 4:
            v = jnp.where(jnp.logical_or(low, high), up, v)
        else:
            down = pltpu.roll(pltpu.roll(v, 8 - bit, 0), 16 * bit, 1)
            v = jnp.where(low, up, jnp.where(high, down, v))
    return v


def tile(q):
    return slice(128 * q, 128 * q + 128)


def splat(table_ref, d, field):
    return table_ref[pl.ds(d * FIELDS + field, 8, stride=0), :]


def by_date(dates, one, carry):
    def body(n, carry):
        for u in range(UNROLL):
            carry = one(n * UNROLL + u, carry)
        return carry

    return lax.fori_loop(0, dates // UNROLL, body, carry)


def form_moments(dates, load, w_ref, table_ref, s_ref, out_refs, ready, done):
    masks = flip_masks()
    zero = jnp.zeros((8, 128), F32)

    def put(row, q, v):
        for (first, count), out_ref in zip(PIECES, out_refs):
            if first <= row < first + count:
                out_ref[pl.ds(q * 8 * count + row - first, 8, stride=count), :] = v

    for first in range(0, EXTRA_S, 11):
        fields = list(range(first, min(first + 11, EXTRA_S)))

        def one(d, acc):
            acc = list(acc)
            w = [w_ref[d, :, tile(q)] for q in range(TILES)]
            for n, e in enumerate(fields):
                x = splat(table_ref, d, e) if e else None
                for q in range(TILES):
                    acc[n * TILES + q] = acc[n * TILES + q] + (x * w[q] if e else w[q])
            return tuple(acc)

        acc = by_date(dates, one, (zero,) * (len(fields) * TILES))
        for n, e in enumerate(fields):
            for q in range(TILES):
                put(extra_row(e), q, flip(acc[n * TILES + q], masks))
    done(0)
    for b in range(BANDS):
        ready(b)

        def one(d, carry):
            acc, square = list(carry[0]), list(carry[1])
            wy = []
            for q in range(TILES):
                y = load(b, d, q)
                v = w_ref[d, :, tile(q)] * y
                square[q] = square[q] + v * y
                wy.append(v)
            for k in range(TERMS):
                x = splat(table_ref, d, COLUMN[k]) if k else None
                for q in range(TILES):
                    acc[k * TILES + q] = acc[k * TILES + q] + (x * wy[q] if k else wy[q])
            return tuple(acc), tuple(square)

        acc, square = by_date(dates, one, ((zero,) * (TERMS * TILES), (zero,) * TILES))
        for k in range(TERMS):
            for q in range(TILES):
                put(8 * b + k, q, flip(acc[k * TILES + q], masks))
        for q in range(TILES):
            total = square[q] if b == 0 else s_ref[:, tile(q)] + square[q]
            if b < BANDS - 1:
                s_ref[:, tile(q)] = total
            else:
                put(extra_row(EXTRA_S), q, flip(total, masks))
                for row in range(extra_row(EXTRA_S) + 1, 64):
                    put(row, q, zero)
        for n, (first, count) in enumerate(PIECES):
            if n and 8 * b + 8 == min(first + count, 8 * BANDS):
                done(n)


def form_residuals(dates, obs_ref, mask_ref, table_ref, block_ref, r_ref, w_ref, smooth_ready):
    masks = flip_masks()

    def get(row, q):
        return flip(block_ref[pl.ds(q * 8 * BLOCK + row, 8, stride=BLOCK), :], masks)

    for b in range(BANDS):
        beta = [[get(8 * b + k, q) for q in range(TILES)] for k in range(TERMS)]

        def one(d, carry):
            x = [splat(table_ref, d, COLUMN[k]) if k else None for k in range(TERMS)]
            for q in range(TILES):
                fit = beta[0][q]
                for k in range(1, TERMS):
                    fit = fit + x[k] * beta[k][q]
                r = obs_ref[b, d, :, tile(q)].astype(F32) - fit
                r_ref[b, d, :, tile(q)] = r
                if b == 0:
                    w_ref[d, :, tile(q)] = r * r
                else:
                    w_ref[d, :, tile(q)] = w_ref[d, :, tile(q)] + r * r
            return carry

        by_date(dates, one, 0)
    smooth_ready()
    scale = [1.0 / (float(BANDS) * (TUKEY * TUKEY) * (get(8 * BANDS, q) + EPS)) for q in range(TILES)]

    def weigh(d, carry):
        for q in range(TILES):
            left = 1.0 - jnp.minimum(w_ref[d, :, tile(q)] * scale[q], 1.0)
            w_ref[d, :, tile(q)] = mask_ref[d, :, tile(q)] * left * left
        return carry

    by_date(dates, weigh, 0)


def copy_to(src, dst, send, recv, space, date):
    return pltpu.make_async_remote_copy(
        src_ref=src, dst_ref=dst, send_sem=send, recv_sem=recv, device_id=(space, date), device_id_type=MESH
    )


def place():
    s, j = lax.axis_index("space"), lax.axis_index("date")
    return s, j, j // ZS, lax.rem(j, ZS)


def wrap(value, count):
    return lax.rem(value + count, count)


def greet():
    s, j, x, z = place()
    sem = pltpu.get_barrier_semaphore()
    targets = [(s, x * ZS + wrap(z + h, ZS)) for h in (1, -1, 2, -2, 3, -3, 4, -4)] + [(s, (1 - x) * ZS + z)]
    targets += [(wrap(s + a, 16), wrap(j + b, SHARDS)) for a, b in NEIGHBOURS]
    for target in targets:
        pl.semaphore_signal(sem, inc=1, device_id=target, device_id_type=MESH)
    return sem, len(targets)


class Reduction:
    def __init__(self, mom_refs, slot_ref, mine_ref, sems, plan):
        self.mom, self.slot, self.mine, self.plan = mom_refs, slot_ref, mine_ref, plan
        self.send, self.recv = sems
        self.s, self.j, self.x, self.z = place()

    def length(self, n, chain):
        _, first, stride = CHAINS[n][chain]
        return (first + stride - 1) // stride

    def rows(self, n, chain, step):
        way, first, stride = CHAINS[n][chain]
        count = PIECES[n][1]
        return pl.ds(pl.multiple_of(wrap(self.z + way * (first - stride * step), ZS) * count, 8), count)

    def place_of(self, n, chain, step):
        return self.slot.at[chain, step, pl.ds(*PIECES[n])]

    def hop(self, n, chain, step):
        way, first, stride = CHAINS[n][chain]
        reach = min(stride, first - stride * step)
        source = self.mom[n].at[self.rows(n, chain, 0)] if step == 0 else self.place_of(n, chain, step - 1)
        return copy_to(
            source, self.place_of(n, chain, step), self.send.at[chain, step, n], self.recv.at[chain, step, n],
            self.s, self.x * ZS + wrap(self.z + way * reach, ZS),
        )

    def step(self, n, step):
        for chain in range(len(CHAINS[n])):
            if step >= self.length(n, chain):
                continue
            if step:
                self.hop(n, chain, step - 1).wait_recv()
                here = self.place_of(n, chain, step - 1)
                here[...] = here[...] + self.mom[n][self.rows(n, chain, step), :]
            self.hop(n, chain, step).start()

    def finish(self, n):
        first, count = PIECES[n]
        total = self.mom[n][pl.ds(pl.multiple_of(self.z * count, 8), count), :]
        for chain in range(len(CHAINS[n])):
            last = self.length(n, chain) - 1
            self.hop(n, chain, last).wait_recv()
            total = total + self.slot[chain, last, pl.ds(first, count), :]
        self.mine[pl.ds(first, count), :] = total

    def advance(self, stage):
        for n, step in self.plan[stage]:
            if step == max(self.length(n, chain) for chain in range(len(CHAINS[n]))):
                self.finish(n)
            else:
                self.step(n, step)

    def run(self):
        self.advance(len(PIECES))

    def drain(self):
        for n in range(len(PIECES)):
            for chain in range(len(CHAINS[n])):
                for step in range(self.length(n, chain)):
                    self.hop(n, chain, step).wait_send()


class Spread:
    def __init__(self, block_ref, sems):
        self.block = block_ref
        self.send, self.recv = sems
        self.s, self.j, self.x, self.z = place()

    def piece(self, owner, n):
        first, count = PARTS[n]
        return self.block.at[pl.ds(pl.multiple_of(wrap(owner + ZS, ZS) * BLOCK + first, 8), count)]

    def offset(self, n, chain, step):
        way, first, _, stride = SPREADS[n][chain]
        return 0 if step == 0 else way * (first + stride * (step - 1))

    def hop(self, n, chain, step):
        way, first, _, stride = SPREADS[n][chain]
        reach = first if step == 0 else stride
        piece = self.piece(self.z - self.offset(n, chain, step), n)
        return copy_to(
            piece, piece, self.send.at[chain, step, n], self.recv.at[chain, step, n],
            self.s, self.x * ZS + wrap(self.z + way * reach, ZS),
        )

    def arrival(self, n, chain, step):
        piece = self.piece(self.z - self.offset(n, chain, step + 1), n)
        return copy_to(
            piece, piece, self.send.at[chain, step, n], self.recv.at[chain, step, n], self.s, self.j
        )

    def begin(self, n):
        for chain in range(len(SPREADS[n])):
            self.hop(n, chain, 0).start()

    def relay(self, n, step):
        for chain in range(len(SPREADS[n])):
            if step <= SPREADS[n][chain][2]:
                self.arrival(n, chain, step - 1).wait_recv()
                if step < SPREADS[n][chain][2]:
                    self.hop(n, chain, step).start()

    def drain(self):
        for n in range(len(PARTS)):
            for chain in range(len(SPREADS[n])):
                for step in range(SPREADS[n][chain][2]):
                    self.hop(n, chain, step).wait_send()


def solve(mine_ref, base):
    moment = {}

    def mom(e):
        if e not in moment:
            moment[e] = jnp.broadcast_to(mine_ref[extra_row(e) : extra_row(e) + 1, :], (8, 128))
        return moment[e]

    gram = {}
    for i in range(TERMS):
        for j in range(i, TERMS):
            value = None
            for factor, e in gram_terms(i, j):
                part = mom(e) if factor == 1.0 else factor * mom(e)
                value = part if value is None else value + part
            gram[i, j] = value
    cross = [mine_ref[pl.ds(k, 8, stride=8), :] for k in range(TERMS)]
    work = dict(gram)
    for i in range(TERMS):
        work[i, i] = work[i, i] + 1.0
    right = [cross[k] if base is None else cross[k] - base[k] for k in range(TERMS)]
    inverse, factor = [], {}
    for i in range(TERMS):
        inv = 1.0 / work[i, i]
        inverse.append(inv)
        for r in range(i + 1, TERMS):
            factor[r, i] = work[i, r] * inv
        for r in range(i + 1, TERMS):
            for c in range(r, TERMS):
                work[r, c] = work[r, c] - factor[r, i] * work[i, c]
            right[r] = right[r] - factor[r, i] * right[i]
    answer = [None] * TERMS
    for i in reversed(range(TERMS)):
        value = right[i] * inverse[i]
        for c in range(i + 1, TERMS):
            value = value - factor[c, i] * answer[c]
        answer[i] = value
    lost = None
    for i in range(TERMS):
        image = None
        for c in range(TERMS):
            part = gram[min(i, c), max(i, c)] * answer[c]
            image = part if image is None else image + part
        part = answer[i] * (2.0 * cross[i] - image)
        lost = part if lost is None else lost + part
    sub = lax.broadcasted_iota(jnp.int32, (8, 128), 0)
    lost = jnp.sum(jnp.where(sub < BANDS, lost, 0.0), axis=0, keepdims=True)
    spread = jnp.maximum(mom(EXTRA_S) - jnp.broadcast_to(lost, (8, 128)), 0.0) * (1.0 / BANDS)
    return answer, spread / (1.0 + mom(0))


def swap_halo(variance, own_ref, near_ref, sems):
    send, recv = sems
    s, j, x, z = place()
    own_ref[...] = variance
    copies = []
    for n, (a, b) in enumerate(NEIGHBOURS):
        back = NEIGHBOURS.index((-a, -b))
        copy = copy_to(
            own_ref, near_ref.at[back], send.at[n], recv.at[back], wrap(s + a, 16), wrap(j + b, SHARDS)
        )
        copy.start()
        copies.append(copy)
    return copies


def box_mean(variance, near_ref, copies):
    s, j, x, z = place()
    for copy in copies:
        copy.wait()
    lane = lax.broadcasted_iota(jnp.int32, (8, 128), 1)
    col, row = lane % 16, lane // 16

    def field(a, b):
        if (a, b) == (0, 0):
            return variance
        value = near_ref[NEIGHBOURS.index((a, b))]
        inside = jnp.int32(1)
        if a:
            inside = inside * ((s + a >= 0) & (s + a < 16)).astype(jnp.int32)
        if b:
            inside = inside * ((j + b >= 0) & (j + b < SHARDS)).astype(jnp.int32)
        return jnp.where(jnp.full((8, 128), inside) > 0, value, 0.0)

    across = []
    for a in (-1, 0, 1):
        middle = field(a, 0)
        left = pltpu.roll(field(a, -1), 128 - 16, 1)
        right = pltpu.roll(field(a, 1), 16, 1)
        total = middle
        for step in (1, 2):
            total = total + pltpu.roll(jnp.where(col < step, right, middle), 128 - step, 1)
            total = total + pltpu.roll(jnp.where(col >= 16 - step, left, middle), step, 1)
        across.append(total)
    up, middle, down = across
    total = middle
    for step in (1, 2):
        total = total + pltpu.roll(jnp.where(row < step, down, middle), 128 - 16 * step, 1)
        total = total + pltpu.roll(jnp.where(row >= 8 - step, up, middle), 16 * step, 1)

    def count(index, whole):
        return (jnp.minimum(index + 2, whole - 1) - jnp.maximum(index - 2, 0) + 1).astype(F32)

    return total / (count(s * 8 + row, 128) * count(j * 16 + col, COLS))


def whole(
    dates, days_ref, obs_hbm, valid_hbm, out_ref,
    obs_ref, valid_ref, turned_ref, day_ref, table_ref, mask_ref, w_ref, s_ref, r_ref, block_ref,
    in_sem, trade_send, trade_recv, sp_send, sp_recv, *rest,
):
    s, j, x, z = place()
    own = pl.ds(pl.multiple_of(x * WIDE, 128), WIDE)
    other = pl.ds(pl.multiple_of((1 - x) * WIDE, 128), WIDE)
    early, late = pl.ds(0, dates), pl.ds(dates, dates)
    valid_copies = [
        pltpu.make_async_copy(valid_hbm.at[:, :, cols], valid_ref.at[n], in_sem.at[BANDS + n])
        for n, cols in ((1, other), (0, own))
    ]
    obs_copies = [
        pltpu.make_async_copy(obs_hbm.at[b, :, :, own], obs_ref.at[b, early], in_sem.at[b]) for b in range(BANDS)
    ]
    for copy in valid_copies + obs_copies:
        copy.start()
    barrier, guests = greet()
    partner = (s, (1 - x) * ZS + z)

    def trade(n, src, dst):
        return copy_to(src, dst, trade_send.at[n], trade_recv.at[n], *partner)

    trades = [
        trade(b, obs_hbm.at[b, :, :, other], obs_ref.at[b, late]) for b in range(BANDS)
    ]
    day_trade = trade(BANDS, day_ref.at[early], day_ref.at[late])
    mask_trade = trade(BANDS + 1, turned_ref.at[0], turned_ref.at[1])
    rows = lax.broadcasted_iota(jnp.int32, (dates, 128), 0)
    day = jnp.zeros((dates, 128), F32)
    for d in range(dates):
        day = jnp.where(rows == d, days_ref[d].astype(F32), day)
    day_ref[0:dates, :] = day
    valid_copies[0].wait()

    @pl.loop(0, dates)
    def _(d):
        turned_ref[0, d] = valid_ref[1, d].astype(F32).astype(jnp.bfloat16)

    design_table(dates, 0, day_ref, table_ref)
    pl.semaphore_wait(barrier, guests)
    day_trade.start()
    mask_trade.start()
    for copy in trades:
        copy.start()
    valid_copies[1].wait()

    @pl.loop(0, dates)
    def _(d):
        mask_ref[d] = valid_ref[0, d].astype(F32)

    day_trade.wait_recv()
    design_table(dates, dates, day_ref, table_ref)
    mask_trade.wait_recv()

    @pl.loop(0, dates)
    def _(d):
        mask_ref[dates + d] = turned_ref[1, d].astype(F32)

    reductions, halos = [], []
    for n in range(2):
        part = rest[12 * n : 12 * n + 12]
        reductions.append(Reduction(part[:4], part[4], part[5], part[8:10], (SLOW_PLAN, FAST_PLAN)[n]))
        halos.append((part[6], part[7], part[10:12]))

    def ready(b):
        obs_copies[b].wait()
        trades[b].wait_recv()

    both = 2 * dates
    first, last = reductions
    form_moments(
        both, lambda b, d, q: obs_ref[b, d, :, tile(q)].astype(F32), mask_ref, table_ref, s_ref, first.mom,
        ready, first.advance,
    )
    first.run()
    answer, variance = solve(first.mine, None)
    own_ref, near_ref, halo_sems = halos[0]
    copies = swap_halo(variance, own_ref, near_ref, halo_sems)
    base_row = pl.multiple_of(z * BLOCK, 8)
    for k in range(TERMS):
        block_ref[pl.ds(base_row + k, 8, stride=8), :] = answer[k]
    spread = Spread(block_ref, (sp_send, sp_recv))
    spread.begin(0)
    spread.begin(1)
    spread.relay(0, 1)
    spread.relay(1, 1)
    smooth = box_mean(variance, near_ref, copies)
    block_ref[pl.ds(pl.multiple_of(base_row + 8 * BANDS, 8), 8), :] = smooth
    spread.begin(2)
    for n, step in ((0, 2), (1, 2), (0, 3), (1, 3), (2, 1), (0, 4), (1, 4)):
        spread.relay(n, step)
    form_residuals(
        both, obs_ref, mask_ref, table_ref, block_ref, r_ref, w_ref, lambda: spread.relay(2, 2)
    )
    form_moments(
        both, lambda b, d, q: r_ref[b, d, :, tile(q)], w_ref, table_ref, s_ref, last.mom,
        lambda b: None, last.advance,
    )
    last.run()
    base = [block_ref[pl.ds(base_row + k, 8, stride=8), :] for k in range(TERMS)]
    answer, variance = solve(last.mine, base)
    own_ref, near_ref, halo_sems = halos[1]
    copies = swap_halo(variance, own_ref, near_ref, halo_sems)
    masks = flip_masks()
    for k in range(TERMS):
        turned = flip(base[k] + answer[k], masks)
        for b in range(BANDS):
            out_ref[b * TERMS + k] = (turned if b == 0 else pltpu.roll(turned, 128 - 16 * b, 1))[:, :16]
    spread.drain()
    first.drain()
    last.drain()
    for copy in trades + [day_trade, mask_trade]:
        copy.wait_send()
    smooth = box_mean(variance, near_ref, copies)
    out_ref[BANDS * TERMS] = flip(jnp.sqrt(smooth + EPS), masks)[:, :16]


def part_outputs(out_ref, coef_ref, noise_ref):
    for b in range(BANDS):
        coef_ref[b] = out_ref[b * TERMS : (b + 1) * TERMS]
    noise_ref[...] = out_ref[BANDS * TERMS]


def reduction_scratch():
    ring, eight = pltpu.SemaphoreType.DMA((8, 4, len(PIECES))), pltpu.SemaphoreType.DMA((8,))
    return [
        *[pltpu.VMEM((ZS * count, 128), F32) for _, count in PIECES],
        pltpu.VMEM((8, 4, DEEP, 128), F32),
        pltpu.VMEM((DEEP, 128), F32),
        pltpu.VMEM((8, 128), F32),
        pltpu.VMEM((8, 8, 128), F32),
        ring, ring, eight, eight,
    ]


def on_device(obs, valid, days):
    dates = obs.shape[1]
    spread = pltpu.SemaphoreType.DMA((8, 4, len(PARTS)))
    trade = pltpu.SemaphoreType.DMA((BANDS + 2,))
    out = pl.pallas_call(
        functools.partial(whole, dates),
        out_shape=jax.ShapeDtypeStruct((BANDS * TERMS + 1, ROWS, 16), F32),
        in_specs=[
            pl.BlockSpec(memory_space=pltpu.SMEM),
            pl.BlockSpec(memory_space=pl.ANY),
            pl.BlockSpec(memory_space=pl.ANY),
        ],
        out_specs=pl.BlockSpec(memory_space=pltpu.VMEM),
        scratch_shapes=[
            pltpu.VMEM((BANDS, 2 * dates, ROWS, WIDE), jnp.bfloat16),
            pltpu.VMEM((2, dates, ROWS, WIDE), jnp.int32),
            pltpu.VMEM((2, dates, ROWS, WIDE), jnp.bfloat16),
            pltpu.VMEM((2 * dates, 128), F32),
            pltpu.VMEM((2 * dates * FIELDS, 128), F32),
            pltpu.VMEM((2 * dates, ROWS, WIDE), F32),
            pltpu.VMEM((2 * dates, ROWS, WIDE), F32),
            pltpu.VMEM((ROWS, WIDE), F32),
            pltpu.VMEM((BANDS, 2 * dates, ROWS, WIDE), F32),
            pltpu.VMEM((ZS * BLOCK, 128), F32),
            pltpu.SemaphoreType.DMA((BANDS + 2,)),
            trade, trade, spread, spread,
            *reduction_scratch(),
            *reduction_scratch(),
        ],
        compiler_params=pltpu.CompilerParams(collective_id=0, has_side_effects=True, vmem_limit_bytes=56 << 20),
    )(days, obs, valid)
    return pl.pallas_call(
        part_outputs,
        out_shape=(
            jax.ShapeDtypeStruct((BANDS, TERMS, ROWS, 16), F32),
            jax.ShapeDtypeStruct((ROWS, 16), F32),
        ),
        in_specs=[pl.BlockSpec(memory_space=pltpu.VMEM)],
        out_specs=(pl.BlockSpec(memory_space=pltpu.VMEM), pl.BlockSpec(memory_space=pltpu.VMEM)),
    )(out)


def solution(mesh):
    in_specs = (P(None, "date", "space", None), P("date", "space", None), P("date"))
    out_specs = (P(None, None, "space", "date"), P("space", "date"))
    return jax.shard_map(on_device, mesh=mesh, in_specs=in_specs, out_specs=out_specs, check_vma=False)
```
